512 devices in a mesh: tm: 64 (over x, z), tile: 8 (over y, core).
Axes of the slice: x: 4, y: 4, z: 16, core: 2. Of those that a mesh axis runs over, the one named last changes fastest.
Arguments:
- movie_frames: bfloat16 [64, 1024, 1024], P('tm', None, 'tile'), may hold values from -6 to 6
- patch_weight: bfloat16 [64, 128], replicated, may hold values from -0.75 to 0.75
- depth_weight: bfloat16 [3, 3, 3, 128], replicated, may hold values from -4 to 4
- point_weight: bfloat16 [3, 128, 128], replicated, may hold values from -0.5 to 0.5
- observe_weight: bfloat16 [16, 16, 128, 256], P('tile'), may hold values from -0.03125 to 0.03125
- input_map: float32 [256, 256], replicated, may hold values from -0.375 to 0.375
- mode_decay: float32 [128], replicated, may hold values from 0.86 to 1, as said below
- mode_angle: float32 [128], replicated, may hold values from -0.1 to 0.1
- smooth_decay: float32 [128], replicated, may hold values from 0.86 to 1, as said below
- smooth_angle: float32 [128], replicated, may hold values from -0.1 to 0.1
- readout: float32 [256, 256], replicated, may hold values from -0.375 to 0.375
Outputs:
- latent: float32 [64, 256], P('tm', 'tile')
The draws below stay inside these ranges and needn't reach their ends.
Inputs may be any that keep to these rules, and one draw needn't show every extreme that they name: `mode_decay`: every mode's magnitude per frame lies strictly below one. `smooth_decay`: every mode's gain magnitude per frame lies strictly below one.
All inputs are finite; a program needn't handle non-finite values.
Results may differ from the reference program's by a relative error of at most 0.00075.
Values may be sent and summed in bfloat16 or wider, within the bound.
No kernel may reach another device: no remote copies, remote signals or barrier semaphores. Data moves between devices by JAX's collectives and lax.ppermute only.
A program may use at most 64 MiB of HBM per device.

```python
import jax
import jax.numpy as jnp
from jax import lax

H = 1024
W = 1024
PATCH = 8
POOL = 8
CH = 128
LAYERS = 3
OBS = 256
MODES = 128
LATENT = 256
FRAMES = 64
STATE = 256


def decay_law(key, slow_share):
    kind_key, rate_key = jax.random.split(key)
    slow_mode = jax.random.uniform(kind_key, (MODES,)) < slow_share
    spread = jax.random.uniform(rate_key, (MODES,))
    slow_rate = jnp.exp(jnp.log(0.1) + spread * jnp.log(20.0)) / FRAMES
    fast_rate = jnp.exp(jnp.log(0.05) + spread * jnp.log(3.0))
    return jnp.exp(-jnp.where(slow_mode, slow_rate, fast_rate)).astype(jnp.float32)


def draw_mode_decay(key, part):
    slow_share = 0.5
    return decay_law(jax.random.fold_in(key, 11), slow_share)


def draw_smooth_decay(key, part):
    slow_share = 0.5
    return decay_law(jax.random.fold_in(key, 23), slow_share)


def block_scale(stream_key, shape, cuts, least, top_value):
    loudness, own = 1.0, jax.random.fold_in(stream_key, 6)
    for position, blocks in cuts:
        draws = jnp.exp(jax.random.uniform(jax.random.fold_in(own, position), (blocks,), jnp.float32, least / len(cuts), top_value / len(cuts)))
        loudness = loudness * jnp.repeat(draws, shape[position] // blocks).reshape([-1 if axis == position else 1 for axis in range(len(shape))])
    return loudness


def scatter_about(key, extent, scale, most, shards=(), dtype=jnp.bfloat16):
    entries = jax.random.normal(key, extent, jnp.float32) * scale
    if len(shards) > 0:
        entries = block_scale(key, extent, shards, -0.22, 0.18) * entries
    return jnp.clip(entries, min=-most, max=most).astype(dtype)


def setup_inputs(seed: int = 0) -> dict:
    arg_keys = jax.random.split(jax.random.key(seed), 12)
    movie_frames = scatter_about(arg_keys[0], (FRAMES, H, W), 1.0, 6.0, ((0, 64), (2, 8)))
    patch_weight = scatter_about(arg_keys[1], (PATCH * PATCH, CH), (PATCH * PATCH) ** -0.5, 0.75)
    depth_weight = scatter_about(arg_keys[2], (LAYERS, 3, 3, CH), 2 ** -0.5, 4.0)
    point_weight = scatter_about(arg_keys[3], (LAYERS, CH, CH), CH ** -0.5, 0.5)
    observe_weight = scatter_about(arg_keys[4], (W // (PATCH * POOL), H // (PATCH * POOL), CH, OBS), ((W // (PATCH * POOL)) * (H // (PATCH * POOL)) * CH) ** -0.5, 0.03125, ((0, 8),))
    input_map = scatter_about(arg_keys[5], (STATE, OBS), OBS ** -0.5, 0.375, (), jnp.float32)
    mode_decay = draw_mode_decay(jax.random.fold_in(arg_keys[11], 71), 0)
    mode_angle = jnp.clip(jax.random.uniform(arg_keys[7], (MODES,), jnp.float32, -0.1, 0.1), -0.1, 0.1)
    smooth_decay = draw_smooth_decay(jax.random.fold_in(arg_keys[11], 71), 0)
    smooth_angle = jnp.clip(jax.random.uniform(arg_keys[9], (MODES,), jnp.float32, -0.1, 0.1), -0.1, 0.1)
    readout = scatter_about(arg_keys[10], (LATENT, STATE), STATE ** -0.5, 0.375, (), jnp.float32)
    return {"movie_frames": movie_frames, "patch_weight": patch_weight, "depth_weight": depth_weight, "point_weight": point_weight, "observe_weight": observe_weight, "input_map": input_map, "mode_decay": mode_decay, "mode_angle": mode_angle, "smooth_decay": smooth_decay, "smooth_angle": smooth_angle, "readout": readout}


def encode(single_frame, patch_weight, depth_weight, point_weight):
    grid_rows = single_frame.shape[0] // PATCH
    grid_cols = single_frame.shape[1] // PATCH
    patches = single_frame.reshape(grid_rows, PATCH, grid_cols, PATCH).transpose(0, 2, 1, 3).reshape(grid_rows, grid_cols, PATCH * PATCH)
    hidden = jax.nn.gelu(jnp.dot(patches, patch_weight, preferred_element_type=jnp.float32)).astype(jnp.bfloat16)
    for layer_index in range(LAYERS):
        padded = jnp.pad(hidden, ((1, 1), (1, 1), (0, 0)))
        summed = jnp.zeros(hidden.shape, jnp.float32)
        for row_shift in range(3):
            for col_shift in range(3):
                kernel = depth_weight[layer_index, row_shift, col_shift].astype(jnp.float32)
                summed = summed + padded[row_shift:row_shift + grid_rows, col_shift:col_shift + grid_cols].astype(jnp.float32) * kernel
        depthwise = summed.astype(jnp.bfloat16)
        branch = jax.nn.gelu(jnp.dot(depthwise, point_weight[layer_index], preferred_element_type=jnp.float32))
        hidden = (hidden.astype(jnp.float32) + branch).astype(jnp.bfloat16)
    pooled = lax.optimization_barrier(jnp.mean(hidden.astype(jnp.float32).reshape(grid_rows // POOL, POOL, grid_cols // POOL, POOL, CH), axis=(1, 3))).astype(jnp.bfloat16)
    return pooled.transpose(1, 0, 2).reshape(-1)

def rotate(state, magnitude, cosine, sine):
    real_part = state[..., 0]
    imag_part = state[..., 1]
    return jnp.stack([magnitude * (cosine * real_part - sine * imag_part), magnitude * (sine * real_part + cosine * imag_part)], axis=-1)

def run_chain(inputs, magnitude, cosine, sine, initial, backward):

    def advance(state, element):
        updated = rotate(state, magnitude, cosine, sine) + element
        return (updated, updated)
    final_state, states = lax.scan(advance, initial, inputs, reverse=backward)
    return states

def reference(movie_frames, patch_weight, depth_weight, point_weight, observe_weight, input_map, mode_decay, mode_angle, smooth_decay, smooth_angle, readout):

    def encode_one(single_frame):
        return encode(single_frame, patch_weight, depth_weight, point_weight)
    features = lax.map(encode_one, movie_frames)
    observed = jnp.dot(features, observe_weight.reshape(-1, OBS), preferred_element_type=jnp.float32)
    drive = jnp.dot(observed, input_map.T, precision=lax.Precision.HIGHEST).reshape(FRAMES, MODES, 2)
    drive = drive * jnp.sqrt(1.0 - mode_decay * mode_decay)[:, None]
    zero_state = jnp.zeros((MODES, 2), jnp.float32)
    filtered = run_chain(drive, mode_decay, jnp.cos(mode_angle), jnp.sin(mode_angle), zero_state, False)
    weighted = filtered * jnp.sqrt(1.0 - smooth_decay * smooth_decay)[:, None]
    smoothed = run_chain(weighted, smooth_decay, jnp.cos(smooth_angle), jnp.sin(smooth_angle), zero_state, True)
    return jnp.dot(smoothed.reshape(FRAMES, STATE), readout.T, precision=lax.Precision.HIGHEST)
```

```python
import jax
import jax.numpy as jnp
from jax import lax
from jax.experimental import pallas as pl
from jax.experimental.pallas import tpu as pltpu
from jax.sharding import PartitionSpec as P

PATCH = 8
POOL = 8
LAYERS = 3


def with_halo(x, sides, width):
    for axis, dim in sides:
        size, length = (lax.axis_size(axis), x.shape[dim])
        up = [(i, (i + 1) % size) for i in range(size - 1)]
        down = [(j, i) for i, j in up]
        last = lax.slice_in_dim(x, length - width, length, axis=dim)
        initial = lax.slice_in_dim(x, 0, width, axis=dim)
        before = lax.ppermute(last, axis, up)
        after = lax.ppermute(initial, axis, down)
        x = jnp.concatenate([before, x, after], axis=dim)
    return x


HIGHEST = lax.Precision.HIGHEST


def dot_t(a, b):
    return lax.dot_general(
        a, b, (((1,), (1,)), ((), ())), precision=HIGHEST, preferred_element_type=jnp.float32
    )


def scan_rows(real, imag, mult_real, mult_imag, backward):
    rows = real.shape[0]
    row = lax.broadcasted_iota(jnp.int32, real.shape, 0)
    step = 1
    while step < rows:
        shift = rows - step if backward else step
        kept = row < rows - step if backward else row >= step
        moved_real = jnp.where(kept, pltpu.roll(real, shift, 0), 0.0)
        moved_imag = jnp.where(kept, pltpu.roll(imag, shift, 0), 0.0)
        real, imag = (
            real + mult_real * moved_real - mult_imag * moved_imag,
            imag + mult_imag * moved_real + mult_real * moved_imag,
        )
        mult_real, mult_imag = (
            mult_real * mult_real - mult_imag * mult_imag,
            2.0 * mult_real * mult_imag,
        )
        step *= 2
    return real, imag


def filter_kernel(frame_ref, seen_ref, input_ref, decay_ref, angle_ref, back_decay_ref, back_angle_ref,
                  readout_ref, out_ref):
    modes = decay_ref.shape[1]
    parts = input_ref.shape[1] // seen_ref.shape[1]
    frames = seen_ref.shape[0] // parts
    lanes = seen_ref.shape[1]
    decay, angle = decay_ref[...], angle_ref[...]
    back_decay, back_angle = back_decay_ref[...], back_angle_ref[...]
    gain = jnp.sqrt(1.0 - decay * decay)
    back_gain = jnp.sqrt(1.0 - back_decay * back_decay)
    mode = lax.broadcasted_iota(jnp.int32, (modes, 2 * modes), 0)
    place = lax.broadcasted_iota(jnp.int32, (modes, 2 * modes), 1)
    real_place = (place == 2 * mode).astype(jnp.float32)
    imag_place = (place == 2 * mode + 1).astype(jnp.float32)
    drive = sum(
        dot_t(seen_ref[pl.ds(k, frames, stride=parts), :], input_ref[:, k * lanes : (k + 1) * lanes])
        for k in range(parts)
    )
    real = dot_t(drive, real_place) * gain
    imag = dot_t(drive, imag_place) * gain
    real, imag = scan_rows(real, imag, decay * jnp.cos(angle), decay * jnp.sin(angle), False)
    real, imag = scan_rows(
        real * back_gain,
        imag * back_gain,
        back_decay * jnp.cos(back_angle),
        back_decay * jnp.sin(back_angle),
        True,
    )
    mine = lax.broadcasted_iota(jnp.int32, real.shape, 0) == frame_ref[0]
    real = jnp.sum(jnp.where(mine, real, 0.0), axis=0, keepdims=True)
    imag = jnp.sum(jnp.where(mine, imag, 0.0), axis=0, keepdims=True)
    shares = out_ref.shape[0]
    width = out_ref.shape[1]
    real = jnp.broadcast_to(real, (shares, modes))
    imag = jnp.broadcast_to(imag, (shares, modes))
    laid = jnp.dot(
        real, real_place, precision=HIGHEST
    ) + jnp.dot(imag, imag_place, precision=HIGHEST)
    latent = dot_t(laid, readout_ref[...])
    share = lax.broadcasted_iota(jnp.int32, (shares, width), 0)
    out = latent[:, :width]
    for k in range(1, shares):
        out = jnp.where(share == k, latent[:, k * width : (k + 1) * width], out)
    out_ref[...] = out


def filter_frames(frame, seen, input_map, mode_decay, mode_angle, smooth_decay, smooth_angle, readout, shares):
    vmem = pl.BlockSpec(memory_space=pltpu.VMEM)
    width = readout.shape[0] // shares
    return pl.pallas_call(
        filter_kernel,
        out_shape=jax.ShapeDtypeStruct((shares, width), jnp.float32),
        in_specs=[pl.BlockSpec(memory_space=pltpu.SMEM)] + [vmem] * 7,
        out_specs=vmem,
        name="filter_frames",
    )(
        frame,
        seen,
        input_map,
        mode_decay[None],
        mode_angle[None],
        smooth_decay[None],
        smooth_angle[None],
        readout,
    )


def embed(frames, patch_weight):
    frame_count, height, width = frames.shape
    grid_rows = height // PATCH
    grid_cols = width // PATCH
    patches = (
        frames.reshape(frame_count, grid_rows, PATCH, grid_cols, PATCH)
        .transpose(0, 1, 3, 2, 4)
        .reshape(frame_count, grid_rows, grid_cols, PATCH * PATCH)
    )
    return jax.nn.gelu(jnp.dot(patches, patch_weight, preferred_element_type=jnp.float32)).astype(
        jnp.bfloat16
    )


def conv_layer(hidden, padded, depth_weight, point_weight, layer_index):
    grid_rows = hidden.shape[1]
    grid_cols = hidden.shape[2]
    summed = jnp.zeros(hidden.shape, jnp.float32)
    for row_shift in range(3):
        for col_shift in range(3):
            kernel = depth_weight[layer_index, row_shift, col_shift].astype(jnp.float32)
            summed = (
                summed
                + padded[
                    :, row_shift : row_shift + grid_rows, col_shift : col_shift + grid_cols
                ].astype(jnp.float32)
                * kernel
            )
    depthwise = summed.astype(jnp.bfloat16)
    branch = jax.nn.gelu(
        jnp.dot(depthwise, point_weight[layer_index], preferred_element_type=jnp.float32)
    )
    return (hidden.astype(jnp.float32) + branch).astype(jnp.bfloat16)


def shards(
    movie_frames,
    patch_weight,
    depth_weight,
    point_weight,
    observe_weight,
    input_map,
    mode_decay,
    mode_angle,
    smooth_decay,
    smooth_angle,
    readout,
):
    frame_count, height, width = movie_frames.shape
    grid_rows = height // PATCH
    grid_cols = width // PATCH
    channels = patch_weight.shape[1]
    tile_count = lax.axis_size("tile")
    hidden = embed(movie_frames, patch_weight)
    for layer_index in range(LAYERS):
        widened = with_halo(hidden, (("tile", 2),), 1)
        padded = jnp.pad(widened, ((0, 0), (1, 1), (0, 0), (0, 0)))
        hidden = conv_layer(hidden, padded, depth_weight, point_weight, layer_index)
    pooled = jnp.mean(
        hidden.astype(jnp.float32).reshape(
            frame_count, grid_rows // POOL, POOL, grid_cols // POOL, POOL, channels
        ),
        axis=(2, 4),
    ).astype(jnp.bfloat16)
    features = pooled.transpose(0, 2, 1, 3).reshape(frame_count, -1)
    partial_value = jnp.dot(
        features,
        observe_weight.reshape(-1, observe_weight.shape[-1]),
        preferred_element_type=jnp.float32,
    )
    frames = lax.axis_size("tm")
    seen = lax.all_to_all(
        jnp.broadcast_to(partial_value.reshape(1, -1, 128), (frames, partial_value.shape[1] // 128, 128)),
        "tm",
        0,
        0,
    ).reshape(-1, 128)
    frame = lax.axis_index("tm").astype(jnp.int32)[None]
    shares = filter_frames(
        frame, seen, input_map, mode_decay, mode_angle, smooth_decay, smooth_angle, readout, tile_count
    )
    terms = lax.all_to_all(shares, "tile", 0, 0)
    return jnp.sum(terms, axis=0, keepdims=True)


def solution(mesh):
    placed = (
        P("tm", None, "tile"),
        P(),
        P(),
        P(),
        P("tile", None, None, None),
        P(),
        P(),
        P(),
        P(),
        P(),
        P(),
    )
    return jax.shard_map(
        shards, mesh=mesh, in_specs=placed, out_specs=P("tm", "tile"), check_vma=False
    )
```

```python
import jax
import jax.numpy as jnp
from jax import lax
from jax.experimental import pallas as pl
from jax.experimental.pallas import tpu as pltpu
from jax.sharding import PartitionSpec as P

PATCH = 8
POOL = 8
LAYERS = 3


PAD = 8
EDGE = LAYERS
VMEM = pl.BlockSpec(memory_space=pltpu.VMEM)
CUBIC = 0.044715
ROOT = 0.7978845608028654


def gelu_of_half(y):
    return y + y * jnp.tanh(y * (2.0 * ROOT + (8.0 * ROOT * CUBIC) * (y * y)))


def put_column(ref, at, value):
    rows, lanes = value.shape
    zeros = jnp.zeros((PAD, lanes), ref.dtype)
    ref[at, :PAD, :] = zeros
    ref[at, PAD : PAD + rows, :] = value.astype(ref.dtype)
    ref[at, PAD + rows :, :] = zeros


def embed_kernel(frame_ref, weight_ref, hidden_ref, first_ref, last_ref, wide_ref, spread_ref):
    lanes = frame_ref.shape[2]
    rows = frame_ref.shape[1] // PATCH
    channels = weight_ref.shape[1]
    group = 32
    cells = group // PATCH
    columns = lanes // PATCH
    wide_ref[...] = frame_ref[0].astype(jnp.float32)
    weight = weight_ref[...].astype(jnp.float32) * 0.5
    spread_ref[...] = jnp.zeros(spread_ref.shape, spread_ref.dtype)
    for i in range(PATCH):
        for c in range(cells):
            at = (i * cells + c) * PATCH
            spread_ref[at : at + PATCH, c * channels : (c + 1) * channels] = weight[i * PATCH : (i + 1) * PATCH]
    spread = spread_ref[...].astype(jnp.bfloat16)
    lines = [wide_ref[pl.ds(i, rows, stride=PATCH), :] for i in range(PATCH)]
    lane_group = lax.broadcasted_iota(jnp.int32, (rows, lanes), 1) // group
    per = lanes // group
    for q in range(per):
        halves = []
        for h in range(PATCH // per):
            half = None
            for s in range(per):
                line = lines[h * per + s]
                shift = ((s - q) * group) % lanes
                line = pltpu.roll(line, shift, 1) if shift else line
                half = line if half is None else jnp.where(lane_group == s, line, half)
            halves.append(half.astype(jnp.bfloat16))
        y = jnp.dot(jnp.concatenate(halves, axis=1), spread, preferred_element_type=jnp.float32)
        for c in range(cells):
            value = gelu_of_half(y[:, c * channels : (c + 1) * channels]).astype(jnp.bfloat16)
            at = q * cells + c
            put_column(hidden_ref, at, value)
            if at < EDGE:
                first_ref[at] = value
            if at >= columns - EDGE:
                last_ref[at - (columns - EDGE)] = value


def embed(frames, patch_weight):
    _, height, lanes = frames.shape
    rows, columns, channels = height // PATCH, lanes // PATCH, patch_weight.shape[1]
    edge = jax.ShapeDtypeStruct((EDGE, rows, channels), jnp.bfloat16)
    return pl.pallas_call(
        embed_kernel,
        out_shape=(jax.ShapeDtypeStruct((columns, rows + 2 * PAD, channels), jnp.float32), edge, edge),
        in_specs=[VMEM] * 2,
        out_specs=(VMEM,) * 3,
        scratch_shapes=[
            pltpu.VMEM((height, lanes), jnp.float32),
            pltpu.VMEM((256, 4 * channels), jnp.float32),
        ],
        compiler_params=pltpu.CompilerParams(vmem_limit_bytes=16 << 20),
        name="embed",
    )(frames, patch_weight)


def taps_of(depth_ref, layer):
    return [depth_ref[layer, k // 3, k % 3 : k % 3 + 1, :].astype(jnp.float32) for k in range(9)]


def new_column(left, middle, right, taps, weight):
    rows = middle.shape[0] - 2 * PAD
    total = None
    for dc, ref in enumerate((left, middle, right)):
        for dr in range(3):
            term = ref[PAD - 1 + dr : PAD - 1 + dr + rows, :] * taps[3 * dr + dc]
            total = term if total is None else total + term
    y = jnp.dot(total.astype(jnp.bfloat16), weight, preferred_element_type=jnp.float32)
    return middle[PAD : PAD + rows, :] + gelu_of_half(y)


def inner_kernel(hidden_ref, depth_ref, point_ref, one_ref, two_ref, sum_ref):
    columns = hidden_ref.shape[0]
    taps = [taps_of(depth_ref, layer) for layer in range(LAYERS)]
    weights = [(point_ref[layer].astype(jnp.float32) * 0.5).astype(jnp.bfloat16) for layer in range(LAYERS)]
    for layer, (source, target) in enumerate(((hidden_ref, one_ref), (one_ref, two_ref), (two_ref, None))):
        for at in range(layer + 1, columns - layer - 1):
            value = new_column(
                source.at[at - 1], source.at[at], source.at[at + 1], taps[layer], weights[layer]
            )
            if target is not None:
                put_column(target, at, value)
            elif at in (EDGE, columns // 2):
                sum_ref[at // POOL] = value
            else:
                sum_ref[at // POOL] += value


def outer_kernel(inside_ref, hidden_ref, one_ref, two_ref, sum_ref, first_ref, last_ref, depth_ref, point_ref,
                 pooled_ref, border_ref):
    columns = hidden_ref.shape[0]
    taps = [taps_of(depth_ref, layer) for layer in range(LAYERS)]
    weights = [(point_ref[layer].astype(jnp.float32) * 0.5).astype(jnp.bfloat16) for layer in range(LAYERS)]
    inside = (inside_ref[0].astype(jnp.float32), inside_ref[1].astype(jnp.float32))
    for side in range(2):
        halo = (first_ref, last_ref)[side]
        for k in range(EDGE):
            put_column(border_ref.at[side, 0], k, halo[k].astype(jnp.float32))

    def view(side, level, at):
        if level <= at < columns - level:
            return (hidden_ref, one_ref, two_ref)[level].at[at]
        return border_ref.at[side, level, at + EDGE - level if side == 0 else at - columns + level]

    sums = [sum_ref[0], sum_ref[1]]
    for layer in range(LAYERS):
        for side in range(2):
            for k in range(EDGE):
                at = k - 2 + layer if side == 0 else columns - 1 - layer + k
                value = new_column(
                    view(side, layer, at - 1),
                    view(side, layer, at),
                    view(side, layer, at + 1),
                    taps[layer],
                    weights[layer],
                )
                if layer == LAYERS - 1:
                    sums[side] = sums[side] + value
                else:
                    if at < 0 or at >= columns:
                        value = value * inside[side]
                    put_column(border_ref.at[side, layer + 1], k, value)
    rows = sums[0].shape[0]
    for g in range(2):
        pooled_ref[g] = (
            jnp.sum(sums[g].reshape(rows // POOL, POOL, sums[g].shape[1]), axis=1) * (1.0 / (POOL * POOL))
        ).astype(jnp.bfloat16)


def encode(frames, patch_weight, depth_weight, point_weight):
    size, here = lax.axis_size("tile"), lax.axis_index("tile")
    hidden, first, last = embed(frames, patch_weight)
    up = [(i, i + 1) for i in range(size - 1)]
    before = lax.ppermute(last, "tile", up)
    after = lax.ppermute(first, "tile", [(j, i) for i, j in up])
    columns, padded, channels = hidden.shape
    rows = padded - 2 * PAD
    level = jax.ShapeDtypeStruct(hidden.shape, jnp.float32)
    one, two, total = pl.pallas_call(
        inner_kernel,
        out_shape=(level, level, jax.ShapeDtypeStruct((2, rows, channels), jnp.float32)),
        in_specs=[VMEM] * 3,
        out_specs=(VMEM,) * 3,
        compiler_params=pltpu.CompilerParams(vmem_limit_bytes=16 << 20),
        cost_estimate=pl.CostEstimate(flops=400_000_000, bytes_accessed=4_000_000, transcendentals=0),
        name="inner",
    )(hidden, depth_weight, point_weight)
    inside = jnp.stack([here > 0, here < size - 1]).astype(jnp.int32)
    return pl.pallas_call(
        outer_kernel,
        out_shape=jax.ShapeDtypeStruct((2, rows // POOL, channels), jnp.bfloat16),
        in_specs=[pl.BlockSpec(memory_space=pltpu.SMEM)] + [VMEM] * 8,
        out_specs=VMEM,
        scratch_shapes=[pltpu.VMEM((2, LAYERS, EDGE, padded, channels), jnp.float32)],
        compiler_params=pltpu.CompilerParams(vmem_limit_bytes=20 << 20),
        name="outer",
    )(inside, hidden, one, two, total, before, after, depth_weight, point_weight)


HIGHEST = lax.Precision.HIGHEST


def dot_t(a, b):
    return lax.dot_general(
        a, b, (((1,), (1,)), ((), ())), precision=HIGHEST, preferred_element_type=jnp.float32
    )


def scan_rows(real, imag, mult_real, mult_imag, backward):
    rows = real.shape[0]
    row = lax.broadcasted_iota(jnp.int32, real.shape, 0)
    step = 1
    while step < rows:
        shift = rows - step if backward else step
        kept = row < rows - step if backward else row >= step
        moved_real = jnp.where(kept, pltpu.roll(real, shift, 0), 0.0)
        moved_imag = jnp.where(kept, pltpu.roll(imag, shift, 0), 0.0)
        real, imag = (
            real + mult_real * moved_real - mult_imag * moved_imag,
            imag + mult_imag * moved_real + mult_real * moved_imag,
        )
        mult_real, mult_imag = (
            mult_real * mult_real - mult_imag * mult_imag,
            2.0 * mult_real * mult_imag,
        )
        step *= 2
    return real, imag


def filter_kernel(frame_ref, seen_ref, input_ref, decay_ref, angle_ref, back_decay_ref, back_angle_ref,
                  readout_ref, out_ref):
    modes = decay_ref.shape[1]
    parts = input_ref.shape[1] // seen_ref.shape[1]
    frames = seen_ref.shape[0] // parts
    lanes = seen_ref.shape[1]
    decay, angle = decay_ref[...], angle_ref[...]
    back_decay, back_angle = back_decay_ref[...], back_angle_ref[...]
    gain = jnp.sqrt(1.0 - decay * decay)
    back_gain = jnp.sqrt(1.0 - back_decay * back_decay)
    mode = lax.broadcasted_iota(jnp.int32, (modes, 2 * modes), 0)
    place = lax.broadcasted_iota(jnp.int32, (modes, 2 * modes), 1)
    real_place = (place == 2 * mode).astype(jnp.float32)
    imag_place = (place == 2 * mode + 1).astype(jnp.float32)
    drive = sum(
        dot_t(seen_ref[pl.ds(k, frames, stride=parts), :], input_ref[:, k * lanes : (k + 1) * lanes])
        for k in range(parts)
    )
    real = dot_t(drive, real_place) * gain
    imag = dot_t(drive, imag_place) * gain
    real, imag = scan_rows(real, imag, decay * jnp.cos(angle), decay * jnp.sin(angle), False)
    real, imag = scan_rows(
        real * back_gain,
        imag * back_gain,
        back_decay * jnp.cos(back_angle),
        back_decay * jnp.sin(back_angle),
        True,
    )
    mine = lax.broadcasted_iota(jnp.int32, real.shape, 0) == frame_ref[0]
    real = jnp.sum(jnp.where(mine, real, 0.0), axis=0, keepdims=True)
    imag = jnp.sum(jnp.where(mine, imag, 0.0), axis=0, keepdims=True)
    shares = out_ref.shape[0]
    width = out_ref.shape[1]
    real = jnp.broadcast_to(real, (shares, modes))
    imag = jnp.broadcast_to(imag, (shares, modes))
    laid = jnp.dot(
        real, real_place, precision=HIGHEST
    ) + jnp.dot(imag, imag_place, precision=HIGHEST)
    latent = dot_t(laid, readout_ref[...])
    share = lax.broadcasted_iota(jnp.int32, (shares, width), 0)
    out = latent[:, :width]
    for k in range(1, shares):
        out = jnp.where(share == k, latent[:, k * width : (k + 1) * width], out)
    out_ref[...] = out


def filter_frames(frame, seen, input_map, mode_decay, mode_angle, smooth_decay, smooth_angle, readout, shares):
    vmem = pl.BlockSpec(memory_space=pltpu.VMEM)
    width = readout.shape[0] // shares
    return pl.pallas_call(
        filter_kernel,
        out_shape=jax.ShapeDtypeStruct((shares, width), jnp.float32),
        in_specs=[pl.BlockSpec(memory_space=pltpu.SMEM)] + [vmem] * 7,
        out_specs=vmem,
        compiler_params=pltpu.CompilerParams(vmem_limit_bytes=8 << 20),
        name="filter_frames",
    )(
        frame,
        seen,
        input_map,
        mode_decay[None],
        mode_angle[None],
        smooth_decay[None],
        smooth_angle[None],
        readout,
    )


def shards(
    movie_frames,
    patch_weight,
    depth_weight,
    point_weight,
    observe_weight,
    input_map,
    mode_decay,
    mode_angle,
    smooth_decay,
    smooth_angle,
    readout,
):
    tile_count = lax.axis_size("tile")
    partial_value = jnp.dot(
        encode(movie_frames, patch_weight, depth_weight, point_weight).reshape(1, -1),
        observe_weight.reshape(-1, observe_weight.shape[-1]),
        preferred_element_type=jnp.float32,
    )
    frames = lax.axis_size("tm")
    partial_value, frame = lax.optimization_barrier(
        (partial_value, lax.axis_index("tm").astype(jnp.int32)[None])
    )
    seen = lax.all_to_all(
        jnp.broadcast_to(partial_value.reshape(1, -1, 128), (frames, partial_value.shape[1] // 128, 128)),
        "tm",
        0,
        0,
    ).reshape(-1, 128)
    shares = filter_frames(
        frame, seen, input_map, mode_decay, mode_angle, smooth_decay, smooth_angle, readout, tile_count
    )
    terms = lax.all_to_all(shares, "tile", 0, 0)
    return jnp.sum(terms, axis=0, keepdims=True)


def solution(mesh):
    placed = (
        P("tm", None, "tile"),
        P(),
        P(),
        P(),
        P("tile", None, None, None),
        P(),
        P(),
        P(),
        P(),
        P(),
        P(),
    )
    return jax.shard_map(
        shards, mesh=mesh, in_specs=placed, out_specs=P("tm", "tile"), check_vma=False
    )
```

```python
import jax
import jax.numpy as jnp
from jax import lax
from jax.experimental import pallas as pl
from jax.experimental.pallas import tpu as pltpu
from jax.sharding import PartitionSpec as P

PATCH = 8
POOL = 8
LAYERS = 3


PAD = 8
EDGE = LAYERS
VMEM = pl.BlockSpec(memory_space=pltpu.VMEM)
HBM = pl.BlockSpec(memory_space=pltpu.HBM)
PARTS = 4
CUBIC = 0.044715
ROOT = 0.7978845608028654


def gelu_of_half(y):
    return y + y * jnp.tanh(y * (2.0 * ROOT + (8.0 * ROOT * CUBIC) * (y * y)))


def put_column(ref, at, value):
    rows, lanes = value.shape
    zeros = jnp.zeros((PAD, lanes), ref.dtype)
    ref[at, :PAD, :] = zeros
    ref[at, PAD : PAD + rows, :] = value.astype(ref.dtype)
    ref[at, PAD + rows :, :] = zeros


def embed_kernel(frame_hbm, patch_hbm, depth_hbm, point_hbm, hidden_ref, partner_ref, other_ref, depth_ref,
                 point_ref, frame_ref, weight_ref, first_ref, last_ref, wide_ref, spread_ref, sems):
    height, lanes = frame_ref.shape
    rows = height // PATCH
    channels = weight_ref.shape[1]
    group = 32
    cells = group // PATCH
    columns = lanes // PATCH
    part = height // PARTS
    pieces = [
        pltpu.make_async_copy(
            frame_hbm.at[0, pl.ds(k * part, part), :], frame_ref.at[pl.ds(k * part, part), :], sems.at[k]
        )
        for k in range(PARTS)
    ]
    patch = pltpu.make_async_copy(patch_hbm, weight_ref, sems.at[PARTS])
    depth = pltpu.make_async_copy(depth_hbm, depth_ref, sems.at[PARTS + 1])
    point = pltpu.make_async_copy(point_hbm, point_ref, sems.at[PARTS + 2])
    patch.start()
    for piece in pieces:
        piece.start()
    depth.start()
    point.start()
    spread_ref[...] = jnp.zeros(spread_ref.shape, spread_ref.dtype)
    patch.wait()
    weight = weight_ref[...].astype(jnp.float32) * 0.5
    for i in range(PATCH):
        for c in range(cells):
            at = (i * cells + c) * PATCH
            spread_ref[at : at + PATCH, c * channels : (c + 1) * channels] = weight[i * PATCH : (i + 1) * PATCH]
    spread = spread_ref[...].astype(jnp.bfloat16)
    for k, piece in enumerate(pieces):
        piece.wait()
        wide_ref[pl.ds(k * part, part), :] = frame_ref[pl.ds(k * part, part), :].astype(jnp.float32)
    lines = [wide_ref[pl.ds(i, rows, stride=PATCH), :] for i in range(PATCH)]
    lane_group = lax.broadcasted_iota(jnp.int32, (rows, lanes), 1) // group
    per = lanes // group
    for q in range(per):
        halves = []
        for h in range(PATCH // per):
            half = None
            for s in range(per):
                line = lines[h * per + s]
                shift = ((s - q) * group) % lanes
                line = pltpu.roll(line, shift, 1) if shift else line
                half = line if half is None else jnp.where(lane_group == s, line, half)
            halves.append(half.astype(jnp.bfloat16))
        y = jnp.dot(jnp.concatenate(halves, axis=1), spread, preferred_element_type=jnp.float32)
        for c in range(cells):
            value = gelu_of_half(y[:, c * channels : (c + 1) * channels]).astype(jnp.bfloat16)
            at = q * cells + c
            put_column(hidden_ref, at, value)
            if at < EDGE:
                first_ref[at] = value
            if at >= columns - EDGE:
                last_ref[at - (columns - EDGE)] = value
    odd = lax.rem(lax.axis_index("tile"), 2) == 1
    partner_ref[...] = jnp.where(odd, first_ref[...], last_ref[...])
    other_ref[...] = jnp.where(odd, last_ref[...], first_ref[...])
    depth.wait()
    point.wait()


def embed(frames, patch_weight, depth_weight, point_weight):
    _, height, lanes = frames.shape
    rows, columns, channels = height // PATCH, lanes // PATCH, patch_weight.shape[1]
    edge = jax.ShapeDtypeStruct((EDGE, rows, channels), jnp.bfloat16)
    return pl.pallas_call(
        embed_kernel,
        out_shape=(
            jax.ShapeDtypeStruct((columns, rows + 2 * PAD, channels), jnp.float32),
            edge,
            edge,
            jax.ShapeDtypeStruct(depth_weight.shape, depth_weight.dtype),
            jax.ShapeDtypeStruct(point_weight.shape, point_weight.dtype),
        ),
        in_specs=[HBM] * 4,
        out_specs=(VMEM,) * 5,
        scratch_shapes=[
            pltpu.VMEM((height, lanes), frames.dtype),
            pltpu.VMEM(patch_weight.shape, patch_weight.dtype),
            pltpu.VMEM(edge.shape, edge.dtype),
            pltpu.VMEM(edge.shape, edge.dtype),
            pltpu.VMEM((height, lanes), jnp.float32),
            pltpu.VMEM((256, 4 * channels), jnp.float32),
            pltpu.SemaphoreType.DMA((PARTS + 3,)),
        ],
        compiler_params=pltpu.CompilerParams(vmem_limit_bytes=16 << 20),
        name="embed",
    )(*(pltpu.with_memory_space_constraint(x, pltpu.HBM) for x in (frames, patch_weight, depth_weight, point_weight)))


def taps_of(depth_ref, layer):
    return [depth_ref[layer, k // 3, k % 3 : k % 3 + 1, :].astype(jnp.float32) for k in range(9)]


def new_column(left, middle, right, taps, weight):
    rows = middle.shape[0] - 2 * PAD
    total = None
    for dc, ref in enumerate((left, middle, right)):
        for dr in range(3):
            term = ref[PAD - 1 + dr : PAD - 1 + dr + rows, :] * taps[3 * dr + dc]
            total = term if total is None else total + term
    y = jnp.dot(total.astype(jnp.bfloat16), weight, preferred_element_type=jnp.float32)
    return middle[PAD : PAD + rows, :] + gelu_of_half(y)


def inner_kernel(hidden_ref, depth_ref, point_ref, one_ref, two_ref, sum_ref):
    columns = hidden_ref.shape[0]
    taps = [taps_of(depth_ref, layer) for layer in range(LAYERS)]
    weights = [(point_ref[layer].astype(jnp.float32) * 0.5).astype(jnp.bfloat16) for layer in range(LAYERS)]
    for layer, (source, target) in enumerate(((hidden_ref, one_ref), (one_ref, two_ref), (two_ref, None))):
        for at in range(layer + 1, columns - layer - 1):
            value = new_column(
                source.at[at - 1], source.at[at], source.at[at + 1], taps[layer], weights[layer]
            )
            if target is not None:
                put_column(target, at, value)
            elif at in (EDGE, columns // 2):
                sum_ref[at // POOL] = value
            else:
                sum_ref[at // POOL] += value


def outer_kernel(hidden_ref, one_ref, two_ref, sum_ref, partner_ref, other_ref, depth_ref, point_ref,
                 pooled_ref, border_ref):
    columns = hidden_ref.shape[0]
    taps = [taps_of(depth_ref, layer) for layer in range(LAYERS)]
    weights = [(point_ref[layer].astype(jnp.float32) * 0.5).astype(jnp.bfloat16) for layer in range(LAYERS)]
    here, size = lax.axis_index("tile"), lax.axis_size("tile")
    odd = lax.rem(here, 2)
    inside = ((here > 0).astype(jnp.float32), (here < size - 1).astype(jnp.float32))
    for halo, side in ((partner_ref, 1 - odd), (other_ref, odd)):
        for k in range(EDGE):
            put_column(border_ref.at[side, 0], k, halo[k].astype(jnp.float32))

    def view(side, level, at):
        if level <= at < columns - level:
            return (hidden_ref, one_ref, two_ref)[level].at[at]
        return border_ref.at[side, level, at + EDGE - level if side == 0 else at - columns + level]

    sums = [sum_ref[0], sum_ref[1]]
    for layer in range(LAYERS):
        for side in range(2):
            for k in range(EDGE):
                at = k - 2 + layer if side == 0 else columns - 1 - layer + k
                value = new_column(
                    view(side, layer, at - 1),
                    view(side, layer, at),
                    view(side, layer, at + 1),
                    taps[layer],
                    weights[layer],
                )
                if layer == LAYERS - 1:
                    sums[side] = sums[side] + value
                else:
                    if at < 0 or at >= columns:
                        value = value * inside[side]
                    put_column(border_ref.at[side, layer + 1], k, value)
    rows = sums[0].shape[0]
    for g in range(2):
        pooled_ref[g] = (
            jnp.sum(sums[g].reshape(rows // POOL, POOL, sums[g].shape[1]), axis=1) * (1.0 / (POOL * POOL))
        ).astype(jnp.bfloat16)


def encode(frames, patch_weight, depth_weight, point_weight):
    size = lax.axis_size("tile")
    hidden, partner, other, depth_weight, point_weight = embed(
        frames, patch_weight, depth_weight, point_weight
    )
    partner = lax.ppermute(partner, "tile", [(i, i ^ 1) for i in range(size)])
    pairs = [(i, i + 1) for i in range(1, size - 1, 2)]
    other = lax.ppermute(other, "tile", pairs + [(j, i) for i, j in pairs])
    columns, padded, channels = hidden.shape
    rows = padded - 2 * PAD
    level = jax.ShapeDtypeStruct(hidden.shape, jnp.float32)
    one, two, total = pl.pallas_call(
        inner_kernel,
        out_shape=(level, level, jax.ShapeDtypeStruct((2, rows, channels), jnp.float32)),
        in_specs=[VMEM] * 3,
        out_specs=(VMEM,) * 3,
        compiler_params=pltpu.CompilerParams(vmem_limit_bytes=16 << 20),
        cost_estimate=pl.CostEstimate(flops=400_000_000, bytes_accessed=4_000_000, transcendentals=0),
        name="inner",
    )(hidden, depth_weight, point_weight)
    return pl.pallas_call(
        outer_kernel,
        out_shape=jax.ShapeDtypeStruct((2, rows // POOL, channels), jnp.bfloat16),
        in_specs=[VMEM] * 8,
        out_specs=VMEM,
        scratch_shapes=[pltpu.VMEM((2, LAYERS, EDGE, padded, channels), jnp.float32)],
        compiler_params=pltpu.CompilerParams(vmem_limit_bytes=20 << 20),
        name="outer",
    )(hidden, one, two, total, partner, other, depth_weight, point_weight)


def in_two(x):
    high = x.astype(jnp.bfloat16)
    return high, (x - high.astype(jnp.float32)).astype(jnp.bfloat16)


def dot_t(a, b):
    def dot(u, v):
        return lax.dot_general(u, v, (((1,), (1,)), ((), ())), preferred_element_type=jnp.float32)

    a_high, a_low = in_two(a)
    b_high, b_low = in_two(b)
    return dot(a_low, b_high) + dot(a_high, b_low) + dot(a_high, b_high)


def lanes_at(x, index):
    return jnp.take_along_axis(x, index, axis=1, mode="promise_in_bounds")


def scan_rows(real, imag, mult_real, mult_imag, backward):
    rows = real.shape[0]
    row = lax.broadcasted_iota(jnp.int32, real.shape, 0)
    step = 1
    while step < rows:
        shift = rows - step if backward else step
        kept = row < rows - step if backward else row >= step
        moved_real = jnp.where(kept, pltpu.roll(real, shift, 0), 0.0)
        moved_imag = jnp.where(kept, pltpu.roll(imag, shift, 0), 0.0)
        real, imag = (
            real + mult_real * moved_real - mult_imag * moved_imag,
            imag + mult_imag * moved_real + mult_real * moved_imag,
        )
        mult_real, mult_imag = (
            mult_real * mult_real - mult_imag * mult_imag,
            2.0 * mult_real * mult_imag,
        )
        step *= 2
    return real, imag


def filter_kernel(seen_ref, input_ref, decay_ref, angle_ref, back_decay_ref, back_angle_ref, readout_ref, out_ref):
    modes = decay_ref.shape[1]
    parts = input_ref.shape[1] // seen_ref.shape[1]
    frames = seen_ref.shape[0] // parts
    decay, angle = decay_ref[...], angle_ref[...]
    back_decay, back_angle = back_decay_ref[...], back_angle_ref[...]
    gain = jnp.sqrt(1.0 - decay * decay)
    back_gain = jnp.sqrt(1.0 - back_decay * back_decay)
    seen = jnp.concatenate([seen_ref[pl.ds(k, frames, stride=parts), :] for k in range(parts)], axis=1)
    drive = dot_t(seen, input_ref[...])
    lower, upper = drive[:, :modes], drive[:, modes:]
    lane = lax.broadcasted_iota(jnp.int32, (frames, modes), 1)
    even = lax.rem(2 * lane, modes)
    in_lower = lane < modes // 2
    real = jnp.where(in_lower, lanes_at(lower, even), lanes_at(upper, even)) * gain
    imag = jnp.where(in_lower, lanes_at(lower, even + 1), lanes_at(upper, even + 1)) * gain
    real, imag = scan_rows(real, imag, decay * jnp.cos(angle), decay * jnp.sin(angle), False)
    real, imag = scan_rows(
        real * back_gain,
        imag * back_gain,
        back_decay * jnp.cos(back_angle),
        back_decay * jnp.sin(back_angle),
        True,
    )
    mine = lax.broadcasted_iota(jnp.int32, real.shape, 0) == lax.axis_index("tm")
    shares = out_ref.shape[0]
    width = out_ref.shape[1]
    real = jnp.broadcast_to(jnp.sum(jnp.where(mine, real, 0.0), axis=0, keepdims=True), (shares, modes))
    imag = jnp.broadcast_to(jnp.sum(jnp.where(mine, imag, 0.0), axis=0, keepdims=True), (shares, modes))
    lane = lax.broadcasted_iota(jnp.int32, (shares, modes), 1)
    mode = lane // 2
    is_real = lane == 2 * mode
    laid = [
        jnp.where(is_real, lanes_at(real, mode + at), lanes_at(imag, mode + at)) for at in (0, modes // 2)
    ]
    latent = dot_t(jnp.concatenate(laid, axis=1), readout_ref[...])
    share = lax.broadcasted_iota(jnp.int32, (shares, width), 0)
    out = latent[:, :width]
    for k in range(1, shares):
        out = jnp.where(share == k, latent[:, k * width : (k + 1) * width], out)
    out_ref[...] = out


def filter_frames(seen, input_map, mode_decay, mode_angle, smooth_decay, smooth_angle, readout, shares):
    width = readout.shape[0] // shares
    return pl.pallas_call(
        filter_kernel,
        out_shape=jax.ShapeDtypeStruct((shares, width), jnp.float32),
        in_specs=[VMEM] * 7,
        out_specs=VMEM,
        compiler_params=pltpu.CompilerParams(vmem_limit_bytes=8 << 20),
        name="filter_frames",
    )(
        seen,
        input_map,
        mode_decay[None],
        mode_angle[None],
        smooth_decay[None],
        smooth_angle[None],
        readout,
    )


def shards(
    movie_frames,
    patch_weight,
    depth_weight,
    point_weight,
    observe_weight,
    input_map,
    mode_decay,
    mode_angle,
    smooth_decay,
    smooth_angle,
    readout,
):
    tile_count = lax.axis_size("tile")
    partial_value = jnp.dot(
        encode(movie_frames, patch_weight, depth_weight, point_weight).reshape(1, -1),
        observe_weight.reshape(-1, observe_weight.shape[-1]),
        preferred_element_type=jnp.float32,
    )
    frames = lax.axis_size("tm")
    partial_value = lax.optimization_barrier(partial_value)
    seen = lax.all_to_all(
        jnp.broadcast_to(partial_value.reshape(1, -1, 128), (frames, partial_value.shape[1] // 128, 128)),
        "tm",
        0,
        0,
    ).reshape(-1, 128)
    shares = filter_frames(
        seen, input_map, mode_decay, mode_angle, smooth_decay, smooth_angle, readout, tile_count
    )
    terms = lax.all_to_all(shares, "tile", 0, 0)
    return jnp.sum(terms, axis=0, keepdims=True)


def solution(mesh):
    placed = (
        P("tm", None, "tile"),
        P(),
        P(),
        P(),
        P("tile", None, None, None),
        P(),
        P(),
        P(),
        P(),
        P(),
        P(),
    )
    return jax.shard_map(
        shards, mesh=mesh, in_specs=placed, out_specs=P("tm", "tile"), check_vma=False
    )
```

```python
import jax
import jax.numpy as jnp
from jax import lax
from jax.experimental import pallas as pl
from jax.experimental.pallas import tpu as pltpu
from jax.sharding import Mesh
from jax.sharding import PartitionSpec as P

PATCH = 8
POOL = 8
LAYERS = 3
BLOCKS = 4


PAD = 8
EDGE = LAYERS
VMEM = pl.BlockSpec(memory_space=pltpu.VMEM)
HBM = pl.BlockSpec(memory_space=pltpu.HBM)
PARTS = 4
CUBIC = 0.044715
ROOT = 0.7978845608028654


def gelu_of_half(y):
    return y + y * jnp.tanh(y * (2.0 * ROOT + (8.0 * ROOT * CUBIC) * (y * y)))


def put_column(ref, at, value):
    rows, lanes = value.shape
    zeros = jnp.zeros((PAD, lanes), ref.dtype)
    ref[at, :PAD, :] = zeros
    ref[at, PAD : PAD + rows, :] = value.astype(ref.dtype)
    ref[at, PAD + rows :, :] = zeros


def embed_kernel(frame_hbm, patch_hbm, depth_hbm, point_hbm, hidden_ref, partner_ref, other_ref, depth_ref,
                 point_ref, frame_ref, weight_ref, first_ref, last_ref, wide_ref, spread_ref, sems):
    height, lanes = frame_ref.shape
    rows = height // PATCH
    channels = weight_ref.shape[1]
    group = 32
    cells = group // PATCH
    columns = lanes // PATCH
    part = height // PARTS
    pieces = [
        pltpu.make_async_copy(
            frame_hbm.at[0, pl.ds(k * part, part), :], frame_ref.at[pl.ds(k * part, part), :], sems.at[k]
        )
        for k in range(PARTS)
    ]
    patch = pltpu.make_async_copy(patch_hbm, weight_ref, sems.at[PARTS])
    depth = pltpu.make_async_copy(depth_hbm, depth_ref, sems.at[PARTS + 1])
    point = pltpu.make_async_copy(point_hbm, point_ref, sems.at[PARTS + 2])
    patch.start()
    for piece in pieces:
        piece.start()
    depth.start()
    point.start()
    spread_ref[...] = jnp.zeros(spread_ref.shape, spread_ref.dtype)
    patch.wait()
    weight = weight_ref[...].astype(jnp.float32) * 0.5
    for i in range(PATCH):
        for c in range(cells):
            at = (i * cells + c) * PATCH
            spread_ref[at : at + PATCH, c * channels : (c + 1) * channels] = weight[i * PATCH : (i + 1) * PATCH]
    spread = spread_ref[...].astype(jnp.bfloat16)
    for k, piece in enumerate(pieces):
        piece.wait()
        wide_ref[pl.ds(k * part, part), :] = frame_ref[pl.ds(k * part, part), :].astype(jnp.float32)
    lines = [wide_ref[pl.ds(i, rows, stride=PATCH), :] for i in range(PATCH)]
    lane_group = lax.broadcasted_iota(jnp.int32, (rows, lanes), 1) // group
    per = lanes // group
    for q in range(per):
        halves = []
        for h in range(PATCH // per):
            half = None
            for s in range(per):
                line = lines[h * per + s]
                shift = ((s - q) * group) % lanes
                line = pltpu.roll(line, shift, 1) if shift else line
                half = line if half is None else jnp.where(lane_group == s, line, half)
            halves.append(half.astype(jnp.bfloat16))
        y = jnp.dot(jnp.concatenate(halves, axis=1), spread, preferred_element_type=jnp.float32)
        for c in range(cells):
            value = gelu_of_half(y[:, c * channels : (c + 1) * channels]).astype(jnp.bfloat16)
            at = q * cells + c
            put_column(hidden_ref, at, value)
            if at < EDGE:
                first_ref[at] = value
            if at >= columns - EDGE:
                last_ref[at - (columns - EDGE)] = value
    odd = lax.rem(lax.axis_index("tile"), 2) == 1
    partner_ref[...] = jnp.where(odd, first_ref[...], last_ref[...])
    other_ref[...] = jnp.where(odd, last_ref[...], first_ref[...])
    depth.wait()
    point.wait()


def embed(frames, patch_weight, depth_weight, point_weight):
    _, height, lanes = frames.shape
    rows, columns, channels = height // PATCH, lanes // PATCH, patch_weight.shape[1]
    edge = jax.ShapeDtypeStruct((EDGE, rows, channels), jnp.bfloat16)
    return pl.pallas_call(
        embed_kernel,
        out_shape=(
            jax.ShapeDtypeStruct((columns, rows + 2 * PAD, channels), jnp.float32),
            edge,
            edge,
            jax.ShapeDtypeStruct(depth_weight.shape, depth_weight.dtype),
            jax.ShapeDtypeStruct(point_weight.shape, point_weight.dtype),
        ),
        in_specs=[HBM] * 4,
        out_specs=(VMEM,) * 5,
        scratch_shapes=[
            pltpu.VMEM((height, lanes), frames.dtype),
            pltpu.VMEM(patch_weight.shape, patch_weight.dtype),
            pltpu.VMEM(edge.shape, edge.dtype),
            pltpu.VMEM(edge.shape, edge.dtype),
            pltpu.VMEM((height, lanes), jnp.float32),
            pltpu.VMEM((256, 4 * channels), jnp.float32),
            pltpu.SemaphoreType.DMA((PARTS + 3,)),
        ],
        compiler_params=pltpu.CompilerParams(vmem_limit_bytes=16 << 20),
        name="embed",
    )(*(pltpu.with_memory_space_constraint(x, pltpu.HBM) for x in (frames, patch_weight, depth_weight, point_weight)))


def taps_of(depth_ref, layer):
    return [depth_ref[layer, k // 3, k % 3 : k % 3 + 1, :].astype(jnp.float32) for k in range(9)]


def new_column(left, middle, right, taps, weight):
    rows = middle.shape[0] - 2 * PAD
    total = None
    for dc, ref in enumerate((left, middle, right)):
        for dr in range(3):
            term = ref[PAD - 1 + dr : PAD - 1 + dr + rows, :] * taps[3 * dr + dc]
            total = term if total is None else total + term
    y = jnp.dot(total.astype(jnp.bfloat16), weight, preferred_element_type=jnp.float32)
    return middle[PAD : PAD + rows, :] + gelu_of_half(y)


def inner_kernel(hidden_ref, depth_ref, point_ref, one_ref, two_ref, sum_ref):
    columns = hidden_ref.shape[0]
    taps = [taps_of(depth_ref, layer) for layer in range(LAYERS)]
    weights = [(point_ref[layer].astype(jnp.float32) * 0.5).astype(jnp.bfloat16) for layer in range(LAYERS)]
    for layer, (source, target) in enumerate(((hidden_ref, one_ref), (one_ref, two_ref), (two_ref, None))):
        for at in range(layer + 1, columns - layer - 1):
            value = new_column(
                source.at[at - 1], source.at[at], source.at[at + 1], taps[layer], weights[layer]
            )
            if target is not None:
                put_column(target, at, value)
            elif at in (EDGE, columns // 2):
                sum_ref[at // POOL] = value
            else:
                sum_ref[at // POOL] += value


def outer_kernel(hidden_ref, one_ref, two_ref, sum_ref, partner_ref, other_ref, depth_ref, point_ref,
                 pooled_ref, border_ref):
    columns = hidden_ref.shape[0]
    taps = [taps_of(depth_ref, layer) for layer in range(LAYERS)]
    weights = [(point_ref[layer].astype(jnp.float32) * 0.5).astype(jnp.bfloat16) for layer in range(LAYERS)]
    here, size = lax.axis_index("tile"), lax.axis_size("tile")
    odd = lax.rem(here, 2)
    inside = ((here > 0).astype(jnp.float32), (here < size - 1).astype(jnp.float32))
    for halo, side in ((partner_ref, 1 - odd), (other_ref, odd)):
        for k in range(EDGE):
            put_column(border_ref.at[side, 0], k, halo[k].astype(jnp.float32))

    def view(side, level, at):
        if level <= at < columns - level:
            return (hidden_ref, one_ref, two_ref)[level].at[at]
        return border_ref.at[side, level, at + EDGE - level if side == 0 else at - columns + level]

    sums = [sum_ref[0], sum_ref[1]]
    for layer in range(LAYERS):
        for side in range(2):
            for k in range(EDGE):
                at = k - 2 + layer if side == 0 else columns - 1 - layer + k
                value = new_column(
                    view(side, layer, at - 1),
                    view(side, layer, at),
                    view(side, layer, at + 1),
                    taps[layer],
                    weights[layer],
                )
                if layer == LAYERS - 1:
                    sums[side] = sums[side] + value
                else:
                    if at < 0 or at >= columns:
                        value = value * inside[side]
                    put_column(border_ref.at[side, layer + 1], k, value)
    rows = sums[0].shape[0]
    for g in range(2):
        pooled_ref[g] = (
            jnp.sum(sums[g].reshape(rows // POOL, POOL, sums[g].shape[1]), axis=1) * (1.0 / (POOL * POOL))
        ).astype(jnp.bfloat16)


def encode(frames, patch_weight, depth_weight, point_weight):
    size = lax.axis_size("tile")
    hidden, partner, other, depth_weight, point_weight = embed(
        frames, patch_weight, depth_weight, point_weight
    )
    pairs = [(i, i + 1) for i in range(1, size - 1, 2)]
    other = lax.ppermute(other, "tile", pairs + [(j, i) for i, j in pairs])
    partner = lax.ppermute(partner, "tile", [(i, i ^ 1) for i in range(size)])
    _, padded, channels = hidden.shape
    rows = padded - 2 * PAD
    level = jax.ShapeDtypeStruct(hidden.shape, jnp.float32)
    one, two, total = pl.pallas_call(
        inner_kernel,
        out_shape=(level, level, jax.ShapeDtypeStruct((2, rows, channels), jnp.float32)),
        in_specs=[VMEM] * 3,
        out_specs=(VMEM,) * 3,
        compiler_params=pltpu.CompilerParams(vmem_limit_bytes=16 << 20),
        cost_estimate=pl.CostEstimate(flops=400_000_000, bytes_accessed=4_000_000, transcendentals=0),
        name="inner",
    )(hidden, depth_weight, point_weight)
    return pl.pallas_call(
        outer_kernel,
        out_shape=jax.ShapeDtypeStruct((2, rows // POOL, channels), jnp.bfloat16),
        in_specs=[VMEM] * 8,
        out_specs=VMEM,
        scratch_shapes=[pltpu.VMEM((2, LAYERS, EDGE, padded, channels), jnp.float32)],
        compiler_params=pltpu.CompilerParams(vmem_limit_bytes=20 << 20),
        name="outer",
    )(hidden, one, two, total, partner, other, depth_weight, point_weight)


def in_two(x):
    high = x.astype(jnp.bfloat16)
    return high, (x - high.astype(jnp.float32)).astype(jnp.bfloat16)


def dot_t(a, b):
    def dot(u, v):
        return lax.dot_general(u, v, (((1,), (1,)), ((), ())), preferred_element_type=jnp.float32)

    a_high, a_low = in_two(a)
    b_high, b_low = in_two(b)
    return dot(a_low, b_high) + dot(a_high, b_low) + dot(a_high, b_high)


def lanes_at(x, index):
    return jnp.take_along_axis(x, index, axis=1, mode="promise_in_bounds")


def scan_rows(real, imag, mult_real, mult_imag, backward):
    rows = real.shape[0]
    row = lax.broadcasted_iota(jnp.int32, real.shape, 0)
    step = 1
    while step < rows:
        shift = rows - step if backward else step
        kept = row < rows - step if backward else row >= step
        moved_real = jnp.where(kept, pltpu.roll(real, shift, 0), 0.0)
        moved_imag = jnp.where(kept, pltpu.roll(imag, shift, 0), 0.0)
        real, imag = (
            real + mult_real * moved_real - mult_imag * moved_imag,
            imag + mult_imag * moved_real + mult_real * moved_imag,
        )
        mult_real, mult_imag = (
            mult_real * mult_real - mult_imag * mult_imag,
            2.0 * mult_real * mult_imag,
        )
        step *= 2
    return real, imag


def filter_kernel(seen_ref, input_ref, decay_ref, angle_ref, back_decay_ref, back_angle_ref, readout_ref, out_ref):
    modes = decay_ref.shape[1]
    parts = input_ref.shape[1] // seen_ref.shape[1]
    frames = seen_ref.shape[0] // parts
    decay, angle = decay_ref[...], angle_ref[...]
    back_decay, back_angle = back_decay_ref[...], back_angle_ref[...]
    gain = jnp.sqrt(1.0 - decay * decay)
    back_gain = jnp.sqrt(1.0 - back_decay * back_decay)
    seen = jnp.concatenate([seen_ref[pl.ds(k, frames, stride=parts), :] for k in range(parts)], axis=1)
    drive = dot_t(seen, input_ref[...])
    lower, upper = drive[:, :modes], drive[:, modes:]
    lane = lax.broadcasted_iota(jnp.int32, (frames, modes), 1)
    even = lax.rem(2 * lane, modes)
    in_lower = lane < modes // 2
    real = jnp.where(in_lower, lanes_at(lower, even), lanes_at(upper, even)) * gain
    imag = jnp.where(in_lower, lanes_at(lower, even + 1), lanes_at(upper, even + 1)) * gain
    blocks = lax.axis_size("x")
    row = lax.broadcasted_iota(jnp.int32, (blocks * frames, modes), 0)
    placed = row // frames == lax.axis_index("x")
    real = jnp.where(placed, jnp.concatenate([real] * blocks, axis=0), 0.0)
    imag = jnp.where(placed, jnp.concatenate([imag] * blocks, axis=0), 0.0)
    real, imag = scan_rows(real, imag, decay * jnp.cos(angle), decay * jnp.sin(angle), False)
    real, imag = scan_rows(
        real * back_gain,
        imag * back_gain,
        back_decay * jnp.cos(back_angle),
        back_decay * jnp.sin(back_angle),
        True,
    )
    length = lax.axis_size("z")
    mine = lax.rem(row, length) == lax.axis_index("z")
    shares, width = out_ref.shape[0] // blocks, out_ref.shape[1]
    real = jnp.sum(jnp.where(mine, real, 0.0).reshape(blocks, length, modes), axis=1)
    imag = jnp.sum(jnp.where(mine, imag, 0.0).reshape(blocks, length, modes), axis=1)
    if blocks < 8:
        real = jnp.concatenate([real] * (8 // blocks), axis=0)
        imag = jnp.concatenate([imag] * (8 // blocks), axis=0)
    lane = lax.broadcasted_iota(jnp.int32, real.shape, 1)
    mode = lane // 2
    is_real = lane == 2 * mode
    laid = [
        jnp.where(is_real, lanes_at(real, mode + at), lanes_at(imag, mode + at)) for at in (0, modes // 2)
    ]
    latent = dot_t(jnp.concatenate(laid, axis=1), readout_ref[...])
    share = lax.broadcasted_iota(jnp.int32, (shares, width), 0)
    for block in range(blocks):
        out = jnp.broadcast_to(latent[block : block + 1, :width], (shares, width))
        for k in range(1, shares):
            out = jnp.where(share == k, latent[block : block + 1, k * width : (k + 1) * width], out)
        out_ref[block * shares : (block + 1) * shares, :] = out


def filter_frames(seen, input_map, mode_decay, mode_angle, smooth_decay, smooth_angle, readout, shares):
    width = readout.shape[0] // shares
    return pl.pallas_call(
        filter_kernel,
        out_shape=jax.ShapeDtypeStruct((lax.axis_size("x") * shares, width), jnp.float32),
        in_specs=[VMEM] * 7,
        out_specs=VMEM,
        compiler_params=pltpu.CompilerParams(vmem_limit_bytes=8 << 20),
        name="filter_frames",
    )(
        seen,
        input_map,
        mode_decay[None],
        mode_angle[None],
        smooth_decay[None],
        smooth_angle[None],
        readout,
    )


def shards(
    movie_frames,
    patch_weight,
    depth_weight,
    point_weight,
    observe_weight,
    input_map,
    mode_decay,
    mode_angle,
    smooth_decay,
    smooth_angle,
    readout,
):
    tile_count = lax.axis_size("tile")
    partial_value = jnp.dot(
        encode(movie_frames, patch_weight, depth_weight, point_weight).reshape(1, -1),
        observe_weight.reshape(-1, observe_weight.shape[-1]),
        preferred_element_type=jnp.float32,
    )
    length = lax.axis_size("z")
    partial_value = lax.optimization_barrier(partial_value)
    seen = lax.all_to_all(
        jnp.broadcast_to(partial_value.reshape(1, -1, 128), (length, partial_value.shape[1] // 128, 128)),
        "z",
        0,
        0,
    ).reshape(-1, 128)
    shares = filter_frames(
        seen, input_map, mode_decay, mode_angle, smooth_decay, smooth_angle, readout, tile_count
    )
    terms = lax.all_to_all(shares, ("x", "tile"), 0, 0)
    return jnp.sum(terms, axis=0, keepdims=True)


def solution(mesh):
    grid = Mesh(mesh.devices.reshape(BLOCKS, -1, mesh.shape["tile"]), ("x", "z", "tile"))
    placed = (
        P(("x", "z"), None, "tile"),
        P(),
        P(),
        P(),
        P("tile", None, None, None),
        P(),
        P(),
        P(),
        P(),
        P(),
        P(),
    )
    return jax.shard_map(
        shards, mesh=grid, in_specs=placed, out_specs=P(("x", "z"), "tile"), check_vma=False
    )
```

```python
import jax
import jax.numpy as jnp
from jax import lax
from jax.experimental import pallas as pl
from jax.experimental.pallas import tpu as pltpu
from jax.sharding import Mesh
from jax.sharding import PartitionSpec as P

PATCH = 8
POOL = 8
LAYERS = 3
BLOCKS = 4


PAD = 8
EDGE = LAYERS
VMEM = pl.BlockSpec(memory_space=pltpu.VMEM)
HBM = pl.BlockSpec(memory_space=pltpu.HBM)
PARTS = 4
CUBIC = 0.044715
ROOT = 0.7978845608028654


def gelu_of_half(y):
    return y + y * jnp.tanh(y * (2.0 * ROOT + (8.0 * ROOT * CUBIC) * (y * y)))


def put_column(ref, at, value):
    rows, lanes = value.shape
    zeros = jnp.zeros((PAD, lanes), ref.dtype)
    ref[at, :PAD, :] = zeros
    ref[at, PAD : PAD + rows, :] = value.astype(ref.dtype)
    ref[at, PAD + rows :, :] = zeros


def put_shifted(column, target):
    half = target.shape[1]
    for dr in range(3):
        at = PAD - 1 + dr
        target[dr] = jnp.concatenate(
            [column[at : at + half, :], column[at + half : at + 2 * half, :]], axis=1
        ).astype(target.dtype)


def embed_kernel(frame_hbm, patch_hbm, depth_hbm, point_hbm, hidden_ref, partner_ref, other_ref, depth_ref,
                 point_ref, frame_ref, weight_ref, first_ref, last_ref, wide_ref, spread_ref, sems):
    height, lanes = frame_ref.shape
    rows = height // PATCH
    channels = weight_ref.shape[1]
    group = 32
    cells = group // PATCH
    columns = lanes // PATCH
    part = height // PARTS
    pieces = [
        pltpu.make_async_copy(
            frame_hbm.at[0, pl.ds(k * part, part), :], frame_ref.at[pl.ds(k * part, part), :], sems.at[k]
        )
        for k in range(PARTS)
    ]
    patch = pltpu.make_async_copy(patch_hbm, weight_ref, sems.at[PARTS])
    depth = pltpu.make_async_copy(depth_hbm, depth_ref, sems.at[PARTS + 1])
    point = pltpu.make_async_copy(point_hbm, point_ref, sems.at[PARTS + 2])
    patch.start()
    for piece in pieces:
        piece.start()
    depth.start()
    point.start()
    spread_ref[...] = jnp.zeros(spread_ref.shape, spread_ref.dtype)
    patch.wait()
    weight = weight_ref[...].astype(jnp.float32) * 0.5
    for i in range(PATCH):
        for c in range(cells):
            at = (i * cells + c) * PATCH
            spread_ref[at : at + PATCH, c * channels : (c + 1) * channels] = weight[i * PATCH : (i + 1) * PATCH]
    spread = spread_ref[...].astype(jnp.bfloat16)
    for k, piece in enumerate(pieces):
        piece.wait()
        wide_ref[pl.ds(k * part, part), :] = frame_ref[pl.ds(k * part, part), :].astype(jnp.float32)
    lines = [wide_ref[pl.ds(i, rows, stride=PATCH), :] for i in range(PATCH)]
    lane_group = lax.broadcasted_iota(jnp.int32, (rows, lanes), 1) // group
    per = lanes // group
    for q in range(per):
        halves = []
        for h in range(PATCH // per):
            half = None
            for s in range(per):
                line = lines[h * per + s]
                shift = ((s - q) * group) % lanes
                line = pltpu.roll(line, shift, 1) if shift else line
                half = line if half is None else jnp.where(lane_group == s, line, half)
            halves.append(half.astype(jnp.bfloat16))
        y = jnp.dot(jnp.concatenate(halves, axis=1), spread, preferred_element_type=jnp.float32)
        for c in range(cells):
            value = gelu_of_half(y[:, c * channels : (c + 1) * channels]).astype(jnp.bfloat16)
            at = q * cells + c
            put_column(hidden_ref, at, value)
            if at < EDGE:
                first_ref[at] = value
            if at >= columns - EDGE:
                last_ref[at - (columns - EDGE)] = value
    odd = lax.rem(lax.axis_index("tile"), 2) == 1
    partner_ref[...] = jnp.where(odd, first_ref[...], last_ref[...])
    other_ref[...] = jnp.where(odd, last_ref[...], first_ref[...])
    depth.wait()
    point.wait()


def embed(frames, patch_weight, depth_weight, point_weight):
    _, height, lanes = frames.shape
    rows, columns, channels = height // PATCH, lanes // PATCH, patch_weight.shape[1]
    edge = jax.ShapeDtypeStruct((EDGE, rows, channels), jnp.bfloat16)
    return pl.pallas_call(
        embed_kernel,
        out_shape=(
            jax.ShapeDtypeStruct((columns, rows + 2 * PAD, channels), jnp.float32),
            edge,
            edge,
            jax.ShapeDtypeStruct(depth_weight.shape, depth_weight.dtype),
            jax.ShapeDtypeStruct(point_weight.shape, point_weight.dtype),
        ),
        in_specs=[HBM] * 4,
        out_specs=(VMEM,) * 5,
        scratch_shapes=[
            pltpu.VMEM((height, lanes), frames.dtype),
            pltpu.VMEM(patch_weight.shape, patch_weight.dtype),
            pltpu.VMEM(edge.shape, edge.dtype),
            pltpu.VMEM(edge.shape, edge.dtype),
            pltpu.VMEM((height, lanes), jnp.float32),
            pltpu.VMEM((256, 4 * channels), jnp.float32),
            pltpu.SemaphoreType.DMA((PARTS + 3,)),
        ],
        compiler_params=pltpu.CompilerParams(vmem_limit_bytes=16 << 20),
        name="embed",
    )(*(pltpu.with_memory_space_constraint(x, pltpu.HBM) for x in (frames, patch_weight, depth_weight, point_weight)))


def taps_of(depth_ref, layer, half):
    channels = depth_ref.shape[3]
    taps = []
    for k in range(9):
        tap = depth_ref[layer, k // 3, k % 3 : k % 3 + 1, :].astype(jnp.float32)
        taps.append(jnp.broadcast_to(jnp.concatenate([tap, tap], axis=1), (half, 2 * channels)).astype(jnp.bfloat16))
    return taps


def weights_of(point_ref, layer):
    weight = point_ref[layer].astype(jnp.float32) * 0.5
    zero = jnp.zeros_like(weight)
    return jnp.concatenate(
        [jnp.concatenate([weight, zero], axis=1), jnp.concatenate([zero, weight], axis=1)], axis=0
    ).astype(jnp.bfloat16)


def new_column(left, middle, right, here, taps, weight):
    half, channels = middle.shape[1], here.shape[1]
    terms = [ref[dr] * taps[3 * dr + dc] for dc, ref in enumerate((left, middle, right)) for dr in range(3)]
    while len(terms) > 1:
        terms = [sum(terms[k : k + 2][1:], terms[k]) for k in range(0, len(terms), 2)]
    y = gelu_of_half(jnp.dot(terms[0], weight, preferred_element_type=jnp.float32))
    y = jnp.concatenate([y[:, :channels], y[:, channels:]], axis=0)
    return here[PAD : PAD + 2 * half, :] + y


def inner_kernel(hidden_ref, depth_ref, point_ref, one_ref, two_ref, sum_ref, shifted_ref):
    columns = hidden_ref.shape[0]
    rows = 2 * shifted_ref.shape[3]
    taps = [taps_of(depth_ref, layer, rows // 2) for layer in range(LAYERS)]
    weights = [weights_of(point_ref, layer) for layer in range(LAYERS)]
    for at in range(columns):
        put_shifted(hidden_ref.at[at], shifted_ref.at[0, at])
    levels = (hidden_ref, one_ref, two_ref, None)
    for layer in range(LAYERS):
        source, target = levels[layer : layer + 2]
        for at in range(layer + 1, columns - layer - 1):
            value = new_column(
                *(shifted_ref.at[layer, at + dc] for dc in (-1, 0, 1)), source.at[at], taps[layer], weights[layer]
            )
            if target is not None:
                put_column(target, at, value)
                put_shifted(target.at[at], shifted_ref.at[layer + 1, at])
            elif at in (EDGE, columns // 2):
                sum_ref[at // POOL] = value
            else:
                sum_ref[at // POOL] += value


def outer_kernel(hidden_ref, one_ref, two_ref, sum_ref, partner_ref, other_ref, depth_ref, point_ref,
                 pooled_ref, border_ref, shifted_ref):
    columns = hidden_ref.shape[0]
    rows = 2 * shifted_ref.shape[4]
    taps = [taps_of(depth_ref, layer, rows // 2) for layer in range(LAYERS)]
    weights = [weights_of(point_ref, layer) for layer in range(LAYERS)]
    here, size = lax.axis_index("tile"), lax.axis_size("tile")
    odd = lax.rem(here, 2)
    inside = ((here > 0).astype(jnp.float32), (here < size - 1).astype(jnp.float32))
    known = (hidden_ref, one_ref, two_ref)

    def border(side, level, at):
        return at + EDGE - level if side == 0 else at - columns + level

    def shifted(side, level, at):
        return shifted_ref.at[side, level, border(side, level, at) + (0 if side == 0 else 2)]

    for level in range(LAYERS):
        for at in (level, level + 1):
            put_shifted(known[level].at[at], shifted(0, level, at))
            mirror = columns - 1 - at
            put_shifted(known[level].at[mirror], shifted(1, level, mirror))
    for halo, side in ((partner_ref, 1 - odd), (other_ref, odd)):
        for k in range(EDGE):
            put_column(border_ref.at[side, 0], k, halo[k].astype(jnp.float32))
    for side in range(2):
        for k in range(EDGE):
            put_shifted(border_ref.at[side, 0, k], shifted_ref.at[side, 0, k + 2 * side])

    sums = [sum_ref[0], sum_ref[1]]
    for layer in range(LAYERS):
        for side in range(2):
            for k in range(EDGE):
                at = k - 2 + layer if side == 0 else columns - 1 - layer + k
                if layer <= at < columns - layer:
                    source = known[layer].at[at]
                else:
                    source = border_ref.at[side, layer, border(side, layer, at)]
                value = new_column(
                    *(shifted(side, layer, at + dc) for dc in (-1, 0, 1)), source, taps[layer], weights[layer]
                )
                if layer == LAYERS - 1:
                    sums[side] = sums[side] + value
                else:
                    if at < 0 or at >= columns:
                        value = value * inside[side]
                    put_column(border_ref.at[side, layer + 1], k, value)
                    put_shifted(border_ref.at[side, layer + 1, k], shifted(side, layer + 1, at))
    for g in range(2):
        pooled_ref[g] = (
            jnp.sum(sums[g].reshape(rows // POOL, POOL, sums[g].shape[1]), axis=1) * (1.0 / (POOL * POOL))
        ).astype(jnp.bfloat16)


def encode(frames, patch_weight, depth_weight, point_weight):
    size = lax.axis_size("tile")
    hidden, partner, other, depth_weight, point_weight = embed(
        frames, patch_weight, depth_weight, point_weight
    )
    pairs = [(i, i + 1) for i in range(1, size - 1, 2)]
    other = lax.ppermute(other, "tile", pairs + [(j, i) for i, j in pairs])
    partner = lax.ppermute(partner, "tile", [(i, i ^ 1) for i in range(size)])
    columns, padded, channels = hidden.shape
    rows = padded - 2 * PAD
    level = jax.ShapeDtypeStruct(hidden.shape, jnp.float32)
    one, two, total = pl.pallas_call(
        inner_kernel,
        out_shape=(level, level, jax.ShapeDtypeStruct((2, rows, channels), jnp.float32)),
        in_specs=[VMEM] * 3,
        out_specs=(VMEM,) * 3,
        scratch_shapes=[pltpu.VMEM((LAYERS, columns, 3, rows // 2, 2 * channels), jnp.bfloat16)],
        compiler_params=pltpu.CompilerParams(vmem_limit_bytes=16 << 20),
        cost_estimate=pl.CostEstimate(flops=400_000_000, bytes_accessed=4_000_000, transcendentals=0),
        name="inner",
    )(hidden, depth_weight, point_weight)
    return pl.pallas_call(
        outer_kernel,
        out_shape=jax.ShapeDtypeStruct((2, rows // POOL, channels), jnp.bfloat16),
        in_specs=[VMEM] * 8,
        out_specs=VMEM,
        scratch_shapes=[
            pltpu.VMEM((2, LAYERS, EDGE, padded, channels), jnp.float32),
            pltpu.VMEM((2, LAYERS, EDGE + 2, 3, rows // 2, 2 * channels), jnp.bfloat16),
        ],
        compiler_params=pltpu.CompilerParams(vmem_limit_bytes=20 << 20),
        name="outer",
    )(hidden, one, two, total, partner, other, depth_weight, point_weight)


def in_two(x):
    high = x.astype(jnp.bfloat16)
    return high, (x - high.astype(jnp.float32)).astype(jnp.bfloat16)


def dot_t(a, b):
    def dot(u, v):
        return lax.dot_general(u, v, (((1,), (1,)), ((), ())), preferred_element_type=jnp.float32)

    a_high, a_low = in_two(a)
    b_high, b_low = in_two(b)
    return dot(a_low, b_high) + dot(a_high, b_low) + dot(a_high, b_high)


def lanes_at(x, index):
    return jnp.take_along_axis(x, index, axis=1, mode="promise_in_bounds")


def scan_rows(real, imag, mult_real, mult_imag, backward):
    rows = real.shape[0]
    row = lax.broadcasted_iota(jnp.int32, real.shape, 0)
    step = 1
    while step < rows:
        shift = rows - step if backward else step
        kept = row < rows - step if backward else row >= step
        moved_real = jnp.where(kept, pltpu.roll(real, shift, 0), 0.0)
        moved_imag = jnp.where(kept, pltpu.roll(imag, shift, 0), 0.0)
        real, imag = (
            real + mult_real * moved_real - mult_imag * moved_imag,
            imag + mult_imag * moved_real + mult_real * moved_imag,
        )
        mult_real, mult_imag = (
            mult_real * mult_real - mult_imag * mult_imag,
            2.0 * mult_real * mult_imag,
        )
        step *= 2
    return real, imag


def filter_kernel(seen_ref, input_ref, decay_ref, angle_ref, back_decay_ref, back_angle_ref, readout_ref, out_ref):
    modes = decay_ref.shape[1]
    parts = input_ref.shape[1] // seen_ref.shape[1]
    frames = seen_ref.shape[0] // parts
    decay, angle = decay_ref[...], angle_ref[...]
    back_decay, back_angle = back_decay_ref[...], back_angle_ref[...]
    gain = jnp.sqrt(1.0 - decay * decay)
    back_gain = jnp.sqrt(1.0 - back_decay * back_decay)
    seen = jnp.concatenate([seen_ref[pl.ds(k, frames, stride=parts), :] for k in range(parts)], axis=1)
    drive = dot_t(seen, input_ref[...])
    lower, upper = drive[:, :modes], drive[:, modes:]
    lane = lax.broadcasted_iota(jnp.int32, (frames, modes), 1)
    even = lax.rem(2 * lane, modes)
    in_lower = lane < modes // 2
    real = jnp.where(in_lower, lanes_at(lower, even), lanes_at(upper, even)) * gain
    imag = jnp.where(in_lower, lanes_at(lower, even + 1), lanes_at(upper, even + 1)) * gain
    blocks = lax.axis_size("x")
    row = lax.broadcasted_iota(jnp.int32, (blocks * frames, modes), 0)
    placed = row // frames == lax.axis_index("x")
    real = jnp.where(placed, jnp.concatenate([real] * blocks, axis=0), 0.0)
    imag = jnp.where(placed, jnp.concatenate([imag] * blocks, axis=0), 0.0)
    real, imag = scan_rows(real, imag, decay * jnp.cos(angle), decay * jnp.sin(angle), False)
    real, imag = scan_rows(
        real * back_gain,
        imag * back_gain,
        back_decay * jnp.cos(back_angle),
        back_decay * jnp.sin(back_angle),
        True,
    )
    length = lax.axis_size("z")
    mine = lax.rem(row, length) == lax.axis_index("z")
    shares = out_ref.shape[0] // blocks
    width = readout_ref.shape[0] // shares
    real = jnp.sum(jnp.where(mine, real, 0.0).reshape(blocks, length, modes), axis=1)
    imag = jnp.sum(jnp.where(mine, imag, 0.0).reshape(blocks, length, modes), axis=1)
    if blocks < 8:
        real = jnp.concatenate([real] * (8 // blocks), axis=0)
        imag = jnp.concatenate([imag] * (8 // blocks), axis=0)
    lane = lax.broadcasted_iota(jnp.int32, real.shape, 1)
    mode = lane // 2
    is_real = lane == 2 * mode
    laid = [
        jnp.where(is_real, lanes_at(real, mode + at), lanes_at(imag, mode + at)) for at in (0, modes // 2)
    ]
    latent = dot_t(jnp.concatenate(laid, axis=1), readout_ref[...])
    lanes = out_ref.shape[1]
    for k in range(shares):
        at = k * width
        half = latent[:, at // lanes * lanes : (at // lanes + 1) * lanes]
        turn = (-at) % lanes
        out_ref[pl.ds(k, blocks, stride=shares), :] = (pltpu.roll(half, turn, 1) if turn else half)[:blocks]


def filter_frames(seen, input_map, mode_decay, mode_angle, smooth_decay, smooth_angle, readout, shares):
    return pl.pallas_call(
        filter_kernel,
        out_shape=jax.ShapeDtypeStruct((lax.axis_size("x") * shares, seen.shape[1]), jnp.float32),
        in_specs=[VMEM] * 7,
        out_specs=VMEM,
        compiler_params=pltpu.CompilerParams(vmem_limit_bytes=8 << 20),
        name="filter_frames",
    )(
        seen,
        input_map,
        mode_decay[None],
        mode_angle[None],
        smooth_decay[None],
        smooth_angle[None],
        readout,
    )


def shards(
    movie_frames,
    patch_weight,
    depth_weight,
    point_weight,
    observe_weight,
    input_map,
    mode_decay,
    mode_angle,
    smooth_decay,
    smooth_angle,
    readout,
):
    tile_count = lax.axis_size("tile")
    partial_value = jnp.dot(
        encode(movie_frames, patch_weight, depth_weight, point_weight).reshape(1, -1),
        observe_weight.reshape(-1, observe_weight.shape[-1]),
        preferred_element_type=jnp.float32,
    )
    length = lax.axis_size("z")
    partial_value = lax.optimization_barrier(partial_value)
    seen = lax.all_to_all(
        jnp.broadcast_to(partial_value.reshape(1, -1, 128), (length, partial_value.shape[1] // 128, 128)),
        "z",
        0,
        0,
    ).reshape(-1, 128)
    shares = filter_frames(
        seen, input_map, mode_decay, mode_angle, smooth_decay, smooth_angle, readout, tile_count
    )
    terms = lax.all_to_all(shares, ("x", "tile"), 0, 0)
    return jnp.sum(terms, axis=0, keepdims=True)[:, : readout.shape[0] // tile_count]


def solution(mesh):
    grid = Mesh(mesh.devices.reshape(BLOCKS, -1, mesh.shape["tile"]), ("x", "z", "tile"))
    placed = (
        P(("x", "z"), None, "tile"),
        P(),
        P(),
        P(),
        P("tile", None, None, None),
        P(),
        P(),
        P(),
        P(),
        P(),
        P(),
    )
    return jax.shard_map(
        shards, mesh=grid, in_specs=placed, out_specs=P(("x", "z"), "tile"), check_vma=False
    )
```

```python
import jax
import jax.numpy as jnp
from jax import lax
from jax.experimental import pallas as pl
from jax.experimental.pallas import tpu as pltpu
from jax.sharding import Mesh
from jax.sharding import PartitionSpec as P

PATCH = 8
POOL = 8
LAYERS = 3
BLOCKS = 4


def from_middle(size):
    return [(i + size // 2) % size for i in range(size)]


PAD = 8
EDGE = LAYERS
VMEM = pl.BlockSpec(memory_space=pltpu.VMEM)
HBM = pl.BlockSpec(memory_space=pltpu.HBM)
PARTS = 4
CUBIC = 0.044715
ROOT = 0.7978845608028654


def gelu_of_half(y):
    return y + y * jnp.tanh(y * (2.0 * ROOT + (8.0 * ROOT * CUBIC) * (y * y)))


def put_column(ref, at, value):
    rows, lanes = value.shape
    zeros = jnp.zeros((PAD, lanes), ref.dtype)
    ref[at, :PAD, :] = zeros
    ref[at, PAD : PAD + rows, :] = value.astype(ref.dtype)
    ref[at, PAD + rows :, :] = zeros


def put_shifted(column, target):
    half = target.shape[1]
    for dr in range(3):
        at = PAD - 1 + dr
        target[dr] = jnp.concatenate(
            [column[at : at + half, :], column[at + half : at + 2 * half, :]], axis=1
        ).astype(target.dtype)


def embed_kernel(frame_hbm, patch_hbm, depth_hbm, point_hbm, hidden_ref, partner_ref, other_ref, depth_ref,
                 point_ref, frame_ref, weight_ref, first_ref, last_ref, wide_ref, spread_ref, sems):
    height, lanes = frame_ref.shape
    rows = height // PATCH
    channels = weight_ref.shape[1]
    group = 32
    cells = group // PATCH
    columns = lanes // PATCH
    part = height // PARTS
    pieces = [
        pltpu.make_async_copy(
            frame_hbm.at[0, pl.ds(k * part, part), :], frame_ref.at[pl.ds(k * part, part), :], sems.at[k]
        )
        for k in range(PARTS)
    ]
    patch = pltpu.make_async_copy(patch_hbm, weight_ref, sems.at[PARTS])
    depth = pltpu.make_async_copy(depth_hbm, depth_ref, sems.at[PARTS + 1])
    point = pltpu.make_async_copy(point_hbm, point_ref, sems.at[PARTS + 2])
    patch.start()
    for piece in pieces:
        piece.start()
    depth.start()
    point.start()
    spread_ref[...] = jnp.zeros(spread_ref.shape, spread_ref.dtype)
    patch.wait()
    weight = weight_ref[...].astype(jnp.float32) * 0.5
    for i in range(PATCH):
        for c in range(cells):
            at = (i * cells + c) * PATCH
            spread_ref[at : at + PATCH, c * channels : (c + 1) * channels] = weight[i * PATCH : (i + 1) * PATCH]
    spread = spread_ref[...].astype(jnp.bfloat16)
    for k, piece in enumerate(pieces):
        piece.wait()
        wide_ref[pl.ds(k * part, part), :] = frame_ref[pl.ds(k * part, part), :].astype(jnp.float32)
    lines = [wide_ref[pl.ds(i, rows, stride=PATCH), :] for i in range(PATCH)]
    lane_group = lax.broadcasted_iota(jnp.int32, (rows, lanes), 1) // group
    per = lanes // group
    for q in range(per):
        halves = []
        for h in range(PATCH // per):
            half = None
            for s in range(per):
                line = lines[h * per + s]
                shift = ((s - q) * group) % lanes
                line = pltpu.roll(line, shift, 1) if shift else line
                half = line if half is None else jnp.where(lane_group == s, line, half)
            halves.append(half.astype(jnp.bfloat16))
        y = jnp.dot(jnp.concatenate(halves, axis=1), spread, preferred_element_type=jnp.float32)
        for c in range(cells):
            value = gelu_of_half(y[:, c * channels : (c + 1) * channels]).astype(jnp.bfloat16)
            at = q * cells + c
            put_column(hidden_ref, at, value)
            if at < EDGE:
                first_ref[at] = value
            if at >= columns - EDGE:
                last_ref[at - (columns - EDGE)] = value
    odd = lax.rem(lax.axis_index("tile"), 2) == 1
    partner_ref[...] = jnp.where(odd, first_ref[...], last_ref[...])
    other_ref[...] = jnp.where(odd, last_ref[...], first_ref[...])
    depth.wait()
    point.wait()


def embed(frames, patch_weight, depth_weight, point_weight):
    _, height, lanes = frames.shape
    rows, columns, channels = height // PATCH, lanes // PATCH, patch_weight.shape[1]
    edge = jax.ShapeDtypeStruct((EDGE, rows, channels), jnp.bfloat16)
    return pl.pallas_call(
        embed_kernel,
        out_shape=(
            jax.ShapeDtypeStruct((columns, rows + 2 * PAD, channels), jnp.float32),
            edge,
            edge,
            jax.ShapeDtypeStruct(depth_weight.shape, depth_weight.dtype),
            jax.ShapeDtypeStruct(point_weight.shape, point_weight.dtype),
        ),
        in_specs=[HBM] * 4,
        out_specs=(VMEM,) * 5,
        scratch_shapes=[
            pltpu.VMEM((height, lanes), frames.dtype),
            pltpu.VMEM(patch_weight.shape, patch_weight.dtype),
            pltpu.VMEM(edge.shape, edge.dtype),
            pltpu.VMEM(edge.shape, edge.dtype),
            pltpu.VMEM((height, lanes), jnp.float32),
            pltpu.VMEM((256, 4 * channels), jnp.float32),
            pltpu.SemaphoreType.DMA((PARTS + 3,)),
        ],
        compiler_params=pltpu.CompilerParams(vmem_limit_bytes=16 << 20),
        name="embed",
    )(*(pltpu.with_memory_space_constraint(x, pltpu.HBM) for x in (frames, patch_weight, depth_weight, point_weight)))


def taps_of(depth_ref, layer, half):
    channels = depth_ref.shape[3]
    taps = []
    for k in range(9):
        tap = depth_ref[layer, k // 3, k % 3 : k % 3 + 1, :].astype(jnp.float32)
        taps.append(jnp.broadcast_to(jnp.concatenate([tap, tap], axis=1), (half, 2 * channels)).astype(jnp.bfloat16))
    return taps


def weights_of(point_ref, layer):
    weight = point_ref[layer].astype(jnp.float32) * 0.5
    zero = jnp.zeros_like(weight)
    return jnp.concatenate(
        [jnp.concatenate([weight, zero], axis=1), jnp.concatenate([zero, weight], axis=1)], axis=0
    ).astype(jnp.bfloat16)


def new_column(left, middle, right, here, taps, weight):
    half, channels = middle.shape[1], here.shape[1]
    terms = [ref[dr] * taps[3 * dr + dc] for dc, ref in enumerate((left, middle, right)) for dr in range(3)]
    while len(terms) > 1:
        terms = [sum(terms[k : k + 2][1:], terms[k]) for k in range(0, len(terms), 2)]
    y = gelu_of_half(jnp.dot(terms[0], weight, preferred_element_type=jnp.float32))
    y = jnp.concatenate([y[:, :channels], y[:, channels:]], axis=0)
    return here[PAD : PAD + 2 * half, :] + y


def inner_kernel(hidden_ref, depth_ref, point_ref, one_ref, two_ref, sum_ref, shifted_ref):
    columns = hidden_ref.shape[0]
    rows = 2 * shifted_ref.shape[3]
    taps = [taps_of(depth_ref, layer, rows // 2) for layer in range(LAYERS)]
    weights = [weights_of(point_ref, layer) for layer in range(LAYERS)]
    for at in range(columns):
        put_shifted(hidden_ref.at[at], shifted_ref.at[0, at])
    levels = (hidden_ref, one_ref, two_ref, None)
    for layer in range(LAYERS):
        source, target = levels[layer : layer + 2]
        for at in range(layer + 1, columns - layer - 1):
            value = new_column(
                *(shifted_ref.at[layer, at + dc] for dc in (-1, 0, 1)), source.at[at], taps[layer], weights[layer]
            )
            if target is not None:
                put_column(target, at, value)
                put_shifted(target.at[at], shifted_ref.at[layer + 1, at])
            elif at in (EDGE, columns // 2):
                sum_ref[at // POOL] = value
            else:
                sum_ref[at // POOL] += value


def outer_kernel(hidden_ref, one_ref, two_ref, sum_ref, partner_ref, other_ref, depth_ref, point_ref,
                 pooled_ref, border_ref, shifted_ref):
    columns = hidden_ref.shape[0]
    rows = 2 * shifted_ref.shape[4]
    taps = [taps_of(depth_ref, layer, rows // 2) for layer in range(LAYERS)]
    weights = [weights_of(point_ref, layer) for layer in range(LAYERS)]
    here, size = lax.axis_index("tile"), lax.axis_size("tile")
    odd = lax.rem(here, 2)
    inside = ((here > 0).astype(jnp.float32), (here < size - 1).astype(jnp.float32))
    known = (hidden_ref, one_ref, two_ref)

    def border(side, level, at):
        return at + EDGE - level if side == 0 else at - columns + level

    def shifted(side, level, at):
        return shifted_ref.at[side, level, border(side, level, at) + (0 if side == 0 else 2)]

    for level in range(LAYERS):
        for at in (level, level + 1):
            put_shifted(known[level].at[at], shifted(0, level, at))
            mirror = columns - 1 - at
            put_shifted(known[level].at[mirror], shifted(1, level, mirror))
    for halo, side in ((partner_ref, 1 - odd), (other_ref, odd)):
        for k in range(EDGE):
            put_column(border_ref.at[side, 0], k, halo[k].astype(jnp.float32))
    for side in range(2):
        for k in range(EDGE):
            put_shifted(border_ref.at[side, 0, k], shifted_ref.at[side, 0, k + 2 * side])

    sums = [sum_ref[0], sum_ref[1]]
    for layer in range(LAYERS):
        for side in range(2):
            for k in range(EDGE):
                at = k - 2 + layer if side == 0 else columns - 1 - layer + k
                if layer <= at < columns - layer:
                    source = known[layer].at[at]
                else:
                    source = border_ref.at[side, layer, border(side, layer, at)]
                value = new_column(
                    *(shifted(side, layer, at + dc) for dc in (-1, 0, 1)), source, taps[layer], weights[layer]
                )
                if layer == LAYERS - 1:
                    sums[side] = sums[side] + value
                else:
                    if at < 0 or at >= columns:
                        value = value * inside[side]
                    put_column(border_ref.at[side, layer + 1], k, value)
                    put_shifted(border_ref.at[side, layer + 1, k], shifted(side, layer + 1, at))
    for g in range(2):
        pooled_ref[g] = (
            jnp.sum(sums[g].reshape(rows // POOL, POOL, sums[g].shape[1]), axis=1) * (1.0 / (POOL * POOL))
        ).astype(jnp.bfloat16)


def encode(frames, patch_weight, depth_weight, point_weight):
    size = lax.axis_size("tile")
    hidden, partner, other, depth_weight, point_weight = embed(
        frames, patch_weight, depth_weight, point_weight
    )
    pairs = [(i, i + 1) for i in range(1, size - 1, 2)]
    other = lax.ppermute(other, "tile", pairs + [(j, i) for i, j in pairs])
    partner = lax.ppermute(partner, "tile", [(i, i ^ 1) for i in range(size)])
    columns, padded, channels = hidden.shape
    rows = padded - 2 * PAD
    level = jax.ShapeDtypeStruct(hidden.shape, jnp.float32)
    one, two, total = pl.pallas_call(
        inner_kernel,
        out_shape=(level, level, jax.ShapeDtypeStruct((2, rows, channels), jnp.float32)),
        in_specs=[VMEM] * 3,
        out_specs=(VMEM,) * 3,
        scratch_shapes=[pltpu.VMEM((LAYERS, columns, 3, rows // 2, 2 * channels), jnp.bfloat16)],
        compiler_params=pltpu.CompilerParams(vmem_limit_bytes=16 << 20),
        cost_estimate=pl.CostEstimate(flops=400_000_000, bytes_accessed=4_000_000, transcendentals=0),
        name="inner",
    )(hidden, depth_weight, point_weight)
    return pl.pallas_call(
        outer_kernel,
        out_shape=jax.ShapeDtypeStruct((2, rows // POOL, channels), jnp.bfloat16),
        in_specs=[VMEM] * 8,
        out_specs=VMEM,
        scratch_shapes=[
            pltpu.VMEM((2, LAYERS, EDGE, padded, channels), jnp.float32),
            pltpu.VMEM((2, LAYERS, EDGE + 2, 3, rows // 2, 2 * channels), jnp.bfloat16),
        ],
        compiler_params=pltpu.CompilerParams(vmem_limit_bytes=20 << 20),
        name="outer",
    )(hidden, one, two, total, partner, other, depth_weight, point_weight)


def in_two(x):
    high = x.astype(jnp.bfloat16)
    return high, (x - high.astype(jnp.float32)).astype(jnp.bfloat16)


def dot_t(a, b):
    def dot(u, v):
        return lax.dot_general(u, v, (((1,), (1,)), ((), ())), preferred_element_type=jnp.float32)

    a_high, a_low = in_two(a)
    b_high, b_low = in_two(b)
    return dot(a_low, b_high) + dot(a_high, b_low) + dot(a_high, b_high)


def lanes_at(x, index):
    return jnp.take_along_axis(x, index, axis=1, mode="promise_in_bounds")


def scan_rows(real, imag, mult_real, mult_imag, backward):
    rows = real.shape[0]
    row = lax.broadcasted_iota(jnp.int32, real.shape, 0)
    step = 1
    while step < rows:
        shift = rows - step if backward else step
        kept = row < rows - step if backward else row >= step
        moved_real = jnp.where(kept, pltpu.roll(real, shift, 0), 0.0)
        moved_imag = jnp.where(kept, pltpu.roll(imag, shift, 0), 0.0)
        real, imag = (
            real + mult_real * moved_real - mult_imag * moved_imag,
            imag + mult_imag * moved_real + mult_real * moved_imag,
        )
        mult_real, mult_imag = (
            mult_real * mult_real - mult_imag * mult_imag,
            2.0 * mult_real * mult_imag,
        )
        step *= 2
    return real, imag


def filter_kernel(seen_ref, input_ref, decay_ref, angle_ref, back_decay_ref, back_angle_ref, readout_ref, out_ref):
    modes = decay_ref.shape[1]
    parts = input_ref.shape[1] // seen_ref.shape[1]
    frames = seen_ref.shape[0] // parts
    decay, angle = decay_ref[...], angle_ref[...]
    back_decay, back_angle = back_decay_ref[...], back_angle_ref[...]
    gain = jnp.sqrt(1.0 - decay * decay)
    back_gain = jnp.sqrt(1.0 - back_decay * back_decay)
    seen = jnp.concatenate([seen_ref[pl.ds(k, frames, stride=parts), :] for k in range(parts)], axis=1)
    drive = dot_t(seen, input_ref[...])
    lower, upper = drive[:, :modes], drive[:, modes:]
    lane = lax.broadcasted_iota(jnp.int32, (frames, modes), 1)
    even = lax.rem(2 * lane, modes)
    in_lower = lane < modes // 2
    real = jnp.where(in_lower, lanes_at(lower, even), lanes_at(upper, even)) * gain
    imag = jnp.where(in_lower, lanes_at(lower, even + 1), lanes_at(upper, even + 1)) * gain
    real, imag = (pltpu.roll(part, frames // 2, 0) for part in (real, imag))
    blocks = lax.axis_size("x")
    row = lax.broadcasted_iota(jnp.int32, (blocks * frames, modes), 0)
    placed = row // frames == lax.axis_index("x")
    real = jnp.where(placed, jnp.concatenate([real] * blocks, axis=0), 0.0)
    imag = jnp.where(placed, jnp.concatenate([imag] * blocks, axis=0), 0.0)
    real, imag = scan_rows(real, imag, decay * jnp.cos(angle), decay * jnp.sin(angle), False)
    real, imag = scan_rows(
        real * back_gain,
        imag * back_gain,
        back_decay * jnp.cos(back_angle),
        back_decay * jnp.sin(back_angle),
        True,
    )
    length = lax.axis_size("z")
    mine = lax.rem(row, length) == lax.axis_index("z")
    shares = out_ref.shape[0] // blocks
    width = readout_ref.shape[0] // shares
    real = jnp.sum(jnp.where(mine, real, 0.0).reshape(blocks, length, modes), axis=1)
    imag = jnp.sum(jnp.where(mine, imag, 0.0).reshape(blocks, length, modes), axis=1)
    if blocks < 8:
        real = jnp.concatenate([real] * (8 // blocks), axis=0)
        imag = jnp.concatenate([imag] * (8 // blocks), axis=0)
    lane = lax.broadcasted_iota(jnp.int32, real.shape, 1)
    mode = lane // 2
    is_real = lane == 2 * mode
    laid = [
        jnp.where(is_real, lanes_at(real, mode + at), lanes_at(imag, mode + at)) for at in (0, modes // 2)
    ]
    latent = dot_t(jnp.concatenate(laid, axis=1), readout_ref[...])
    lanes = out_ref.shape[1]
    for k in range(shares):
        at = k * width
        half = latent[:, at // lanes * lanes : (at // lanes + 1) * lanes]
        turn = (-at) % lanes
        half = pltpu.roll(half, turn, 1) if turn else half
        place = (k + shares - shares // 2) % shares
        out_ref[pl.ds(place, blocks, stride=shares), :] = half[blocks // 2 : blocks // 2 + blocks]


def filter_frames(seen, input_map, mode_decay, mode_angle, smooth_decay, smooth_angle, readout, shares):
    return pl.pallas_call(
        filter_kernel,
        out_shape=jax.ShapeDtypeStruct((lax.axis_size("x") * shares, seen.shape[1]), jnp.float32),
        in_specs=[VMEM] * 7,
        out_specs=VMEM,
        compiler_params=pltpu.CompilerParams(vmem_limit_bytes=8 << 20),
        name="filter_frames",
    )(
        seen,
        input_map,
        mode_decay[None],
        mode_angle[None],
        smooth_decay[None],
        smooth_angle[None],
        readout,
    )


def shards(
    movie_frames,
    patch_weight,
    depth_weight,
    point_weight,
    observe_weight,
    input_map,
    mode_decay,
    mode_angle,
    smooth_decay,
    smooth_angle,
    readout,
):
    tile_count = lax.axis_size("tile")
    partial_value = jnp.dot(
        encode(movie_frames, patch_weight, depth_weight, point_weight).reshape(1, -1),
        observe_weight.reshape(-1, observe_weight.shape[-1]),
        preferred_element_type=jnp.float32,
    )
    length = lax.axis_size("z")
    partial_value = lax.optimization_barrier(partial_value)
    seen = lax.all_to_all(
        jnp.broadcast_to(partial_value.reshape(1, -1, 128), (length, partial_value.shape[1] // 128, 128)),
        "z",
        0,
        0,
        axis_index_groups=[from_middle(length)],
    ).reshape(-1, 128)
    shares = filter_frames(
        seen, input_map, mode_decay, mode_angle, smooth_decay, smooth_angle, readout, tile_count
    )
    order = [
        x * tile_count + tile for x in from_middle(lax.axis_size("x")) for tile in from_middle(tile_count)
    ]
    terms = lax.all_to_all(shares, ("x", "tile"), 0, 0, axis_index_groups=[order])
    return jnp.sum(terms, axis=0, keepdims=True)[:, : readout.shape[0] // tile_count]


def solution(mesh):
    grid = Mesh(mesh.devices.reshape(BLOCKS, -1, mesh.shape["tile"]), ("x", "z", "tile"))
    placed = (
        P(("x", "z"), None, "tile"),
        P(),
        P(),
        P(),
        P("tile", None, None, None),
        P(),
        P(),
        P(),
        P(),
        P(),
        P(),
    )
    return jax.shard_map(
        shards, mesh=grid, in_specs=placed, out_specs=P(("x", "z"), "tile"), check_vma=False
    )
```

```python
import jax
import jax.numpy as jnp
from jax import lax
from jax.experimental import pallas as pl
from jax.experimental.pallas import tpu as pltpu
from jax.sharding import Mesh
from jax.sharding import PartitionSpec as P

PATCH = 8
POOL = 8
LAYERS = 3
BLOCKS = 4


def led_by(size, first):
    return [first] + [i for i in range(size) if i != first]


def middle_of(blocks, shares):
    return blocks // 2 * shares + shares // 2


PAD = 8
EDGE = LAYERS
VMEM = pl.BlockSpec(memory_space=pltpu.VMEM)
HBM = pl.BlockSpec(memory_space=pltpu.HBM)
PARTS = 4
CUBIC = 0.044715
ROOT = 0.7978845608028654


def gelu_of_half(y):
    return y + y * jnp.tanh(y * (2.0 * ROOT + (8.0 * ROOT * CUBIC) * (y * y)))


def put_column(ref, at, value):
    rows, lanes = value.shape
    zeros = jnp.zeros((PAD, lanes), ref.dtype)
    ref[at, :PAD, :] = zeros
    ref[at, PAD : PAD + rows, :] = value.astype(ref.dtype)
    ref[at, PAD + rows :, :] = zeros


def put_shifted(column, target):
    half = target.shape[1]
    for dr in range(3):
        at = PAD - 1 + dr
        target[dr] = jnp.concatenate(
            [column[at : at + half, :], column[at + half : at + 2 * half, :]], axis=1
        ).astype(target.dtype)


def embed_kernel(frame_hbm, patch_hbm, depth_hbm, point_hbm, hidden_ref, partner_ref, other_ref, depth_ref,
                 point_ref, frame_ref, weight_ref, first_ref, last_ref, wide_ref, spread_ref, sems):
    height, lanes = frame_ref.shape
    rows = height // PATCH
    channels = weight_ref.shape[1]
    group = 32
    cells = group // PATCH
    columns = lanes // PATCH
    part = height // PARTS
    pieces = [
        pltpu.make_async_copy(
            frame_hbm.at[0, pl.ds(k * part, part), :], frame_ref.at[pl.ds(k * part, part), :], sems.at[k]
        )
        for k in range(PARTS)
    ]
    patch = pltpu.make_async_copy(patch_hbm, weight_ref, sems.at[PARTS])
    depth = pltpu.make_async_copy(depth_hbm, depth_ref, sems.at[PARTS + 1])
    point = pltpu.make_async_copy(point_hbm, point_ref, sems.at[PARTS + 2])
    patch.start()
    for piece in pieces:
        piece.start()
    depth.start()
    point.start()
    spread_ref[...] = jnp.zeros(spread_ref.shape, spread_ref.dtype)
    patch.wait()
    weight = weight_ref[...].astype(jnp.float32) * 0.5
    for i in range(PATCH):
        for c in range(cells):
            at = (i * cells + c) * PATCH
            spread_ref[at : at + PATCH, c * channels : (c + 1) * channels] = weight[i * PATCH : (i + 1) * PATCH]
    spread = spread_ref[...].astype(jnp.bfloat16)
    for k, piece in enumerate(pieces):
        piece.wait()
        wide_ref[pl.ds(k * part, part), :] = frame_ref[pl.ds(k * part, part), :].astype(jnp.float32)
    lines = [wide_ref[pl.ds(i, rows, stride=PATCH), :] for i in range(PATCH)]
    lane_group = lax.broadcasted_iota(jnp.int32, (rows, lanes), 1) // group
    per = lanes // group
    for q in range(per):
        halves = []
        for h in range(PATCH // per):
            half = None
            for s in range(per):
                line = lines[h * per + s]
                shift = ((s - q) * group) % lanes
                line = pltpu.roll(line, shift, 1) if shift else line
                half = line if half is None else jnp.where(lane_group == s, line, half)
            halves.append(half.astype(jnp.bfloat16))
        y = jnp.dot(jnp.concatenate(halves, axis=1), spread, preferred_element_type=jnp.float32)
        for c in range(cells):
            value = gelu_of_half(y[:, c * channels : (c + 1) * channels]).astype(jnp.bfloat16)
            at = q * cells + c
            put_column(hidden_ref, at, value)
            if at < EDGE:
                first_ref[at] = value
            if at >= columns - EDGE:
                last_ref[at - (columns - EDGE)] = value
    odd = lax.rem(lax.axis_index("tile"), 2) == 1
    partner_ref[...] = jnp.where(odd, first_ref[...], last_ref[...])
    other_ref[...] = jnp.where(odd, last_ref[...], first_ref[...])
    depth.wait()
    point.wait()


def embed(frames, patch_weight, depth_weight, point_weight):
    _, height, lanes = frames.shape
    rows, columns, channels = height // PATCH, lanes // PATCH, patch_weight.shape[1]
    edge = jax.ShapeDtypeStruct((EDGE, rows, channels), jnp.bfloat16)
    return pl.pallas_call(
        embed_kernel,
        out_shape=(
            jax.ShapeDtypeStruct((columns, rows + 2 * PAD, channels), jnp.float32),
            edge,
            edge,
            jax.ShapeDtypeStruct(depth_weight.shape, depth_weight.dtype),
            jax.ShapeDtypeStruct(point_weight.shape, point_weight.dtype),
        ),
        in_specs=[HBM] * 4,
        out_specs=(VMEM,) * 5,
        scratch_shapes=[
            pltpu.VMEM((height, lanes), frames.dtype),
            pltpu.VMEM(patch_weight.shape, patch_weight.dtype),
            pltpu.VMEM(edge.shape, edge.dtype),
            pltpu.VMEM(edge.shape, edge.dtype),
            pltpu.VMEM((height, lanes), jnp.float32),
            pltpu.VMEM((256, 4 * channels), jnp.float32),
            pltpu.SemaphoreType.DMA((PARTS + 3,)),
        ],
        compiler_params=pltpu.CompilerParams(vmem_limit_bytes=16 << 20),
        name="embed",
    )(*(pltpu.with_memory_space_constraint(x, pltpu.HBM) for x in (frames, patch_weight, depth_weight, point_weight)))


def taps_of(depth_ref, layer, half):
    channels = depth_ref.shape[3]
    taps = []
    for k in range(9):
        tap = depth_ref[layer, k // 3, k % 3 : k % 3 + 1, :].astype(jnp.float32)
        taps.append(jnp.broadcast_to(jnp.concatenate([tap, tap], axis=1), (half, 2 * channels)).astype(jnp.bfloat16))
    return taps


def weights_of(point_ref, layer):
    weight = point_ref[layer].astype(jnp.float32) * 0.5
    zero = jnp.zeros_like(weight)
    return jnp.concatenate(
        [jnp.concatenate([weight, zero], axis=1), jnp.concatenate([zero, weight], axis=1)], axis=0
    ).astype(jnp.bfloat16)


def new_column(left, middle, right, here, taps, weight):
    half, channels = middle.shape[1], here.shape[1]
    terms = [ref[dr] * taps[3 * dr + dc] for dc, ref in enumerate((left, middle, right)) for dr in range(3)]
    while len(terms) > 1:
        terms = [sum(terms[k : k + 2][1:], terms[k]) for k in range(0, len(terms), 2)]
    y = gelu_of_half(jnp.dot(terms[0], weight, preferred_element_type=jnp.float32))
    y = jnp.concatenate([y[:, :channels], y[:, channels:]], axis=0)
    return here[PAD : PAD + 2 * half, :] + y


def inner_kernel(hidden_ref, depth_ref, point_ref, one_ref, two_ref, sum_ref, shifted_ref):
    columns = hidden_ref.shape[0]
    rows = 2 * shifted_ref.shape[3]
    taps = [taps_of(depth_ref, layer, rows // 2) for layer in range(LAYERS)]
    weights = [weights_of(point_ref, layer) for layer in range(LAYERS)]
    for at in range(columns):
        put_shifted(hidden_ref.at[at], shifted_ref.at[0, at])
    levels = (hidden_ref, one_ref, two_ref, None)
    for layer in range(LAYERS):
        source, target = levels[layer : layer + 2]
        for at in range(layer + 1, columns - layer - 1):
            value = new_column(
                *(shifted_ref.at[layer, at + dc] for dc in (-1, 0, 1)), source.at[at], taps[layer], weights[layer]
            )
            if target is not None:
                put_column(target, at, value)
                put_shifted(target.at[at], shifted_ref.at[layer + 1, at])
            elif at in (EDGE, columns // 2):
                sum_ref[at // POOL] = value
            else:
                sum_ref[at // POOL] += value


def outer_kernel(hidden_ref, one_ref, two_ref, sum_ref, partner_ref, other_ref, depth_ref, point_ref,
                 pooled_ref, border_ref, shifted_ref):
    columns = hidden_ref.shape[0]
    rows = 2 * shifted_ref.shape[4]
    taps = [taps_of(depth_ref, layer, rows // 2) for layer in range(LAYERS)]
    weights = [weights_of(point_ref, layer) for layer in range(LAYERS)]
    here, size = lax.axis_index("tile"), lax.axis_size("tile")
    odd = lax.rem(here, 2)
    inside = ((here > 0).astype(jnp.float32), (here < size - 1).astype(jnp.float32))
    known = (hidden_ref, one_ref, two_ref)

    def border(side, level, at):
        return at + EDGE - level if side == 0 else at - columns + level

    def shifted(side, level, at):
        return shifted_ref.at[side, level, border(side, level, at) + (0 if side == 0 else 2)]

    for level in range(LAYERS):
        for at in (level, level + 1):
            put_shifted(known[level].at[at], shifted(0, level, at))
            mirror = columns - 1 - at
            put_shifted(known[level].at[mirror], shifted(1, level, mirror))
    for halo, side in ((partner_ref, 1 - odd), (other_ref, odd)):
        for k in range(EDGE):
            put_column(border_ref.at[side, 0], k, halo[k].astype(jnp.float32))
    for side in range(2):
        for k in range(EDGE):
            put_shifted(border_ref.at[side, 0, k], shifted_ref.at[side, 0, k + 2 * side])

    sums = [sum_ref[0], sum_ref[1]]
    for layer in range(LAYERS):
        for side in range(2):
            for k in range(EDGE):
                at = k - 2 + layer if side == 0 else columns - 1 - layer + k
                if layer <= at < columns - layer:
                    source = known[layer].at[at]
                else:
                    source = border_ref.at[side, layer, border(side, layer, at)]
                value = new_column(
                    *(shifted(side, layer, at + dc) for dc in (-1, 0, 1)), source, taps[layer], weights[layer]
                )
                if layer == LAYERS - 1:
                    sums[side] = sums[side] + value
                else:
                    if at < 0 or at >= columns:
                        value = value * inside[side]
                    put_column(border_ref.at[side, layer + 1], k, value)
                    put_shifted(border_ref.at[side, layer + 1, k], shifted(side, layer + 1, at))
    for g in range(2):
        pooled_ref[g] = (
            jnp.sum(sums[g].reshape(rows // POOL, POOL, sums[g].shape[1]), axis=1) * (1.0 / (POOL * POOL))
        ).astype(jnp.bfloat16)


def encode(frames, patch_weight, depth_weight, point_weight):
    size = lax.axis_size("tile")
    hidden, partner, other, depth_weight, point_weight = embed(
        frames, patch_weight, depth_weight, point_weight
    )
    pairs = [(i, i + 1) for i in range(1, size - 1, 2)]
    other = lax.ppermute(other, "tile", pairs + [(j, i) for i, j in pairs])
    partner = lax.ppermute(partner, "tile", [(i, i ^ 1) for i in range(size)])
    columns, padded, channels = hidden.shape
    rows = padded - 2 * PAD
    level = jax.ShapeDtypeStruct(hidden.shape, jnp.float32)
    one, two, total = pl.pallas_call(
        inner_kernel,
        out_shape=(level, level, jax.ShapeDtypeStruct((2, rows, channels), jnp.float32)),
        in_specs=[VMEM] * 3,
        out_specs=(VMEM,) * 3,
        scratch_shapes=[pltpu.VMEM((LAYERS, columns, 3, rows // 2, 2 * channels), jnp.bfloat16)],
        compiler_params=pltpu.CompilerParams(vmem_limit_bytes=16 << 20),
        cost_estimate=pl.CostEstimate(flops=400_000_000, bytes_accessed=4_000_000, transcendentals=0),
        name="inner",
    )(hidden, depth_weight, point_weight)
    return pl.pallas_call(
        outer_kernel,
        out_shape=jax.ShapeDtypeStruct((2, rows // POOL, channels), jnp.bfloat16),
        in_specs=[VMEM] * 8,
        out_specs=VMEM,
        scratch_shapes=[
            pltpu.VMEM((2, LAYERS, EDGE, padded, channels), jnp.float32),
            pltpu.VMEM((2, LAYERS, EDGE + 2, 3, rows // 2, 2 * channels), jnp.bfloat16),
        ],
        compiler_params=pltpu.CompilerParams(vmem_limit_bytes=20 << 20),
        name="outer",
    )(hidden, one, two, total, partner, other, depth_weight, point_weight)


def in_two(x):
    high = x.astype(jnp.bfloat16)
    return high, (x - high.astype(jnp.float32)).astype(jnp.bfloat16)


def dot_t(a, b):
    def dot(u, v):
        return lax.dot_general(u, v, (((1,), (1,)), ((), ())), preferred_element_type=jnp.float32)

    a_high, a_low = in_two(a)
    b_high, b_low = in_two(b)
    return dot(a_low, b_high) + dot(a_high, b_low) + dot(a_high, b_high)


def lanes_at(x, index):
    return jnp.take_along_axis(x, index, axis=1, mode="promise_in_bounds")


def scan_rows(real, imag, mult_real, mult_imag, backward):
    rows = real.shape[0]
    row = lax.broadcasted_iota(jnp.int32, real.shape, 0)
    step = 1
    while step < rows:
        shift = rows - step if backward else step
        kept = row < rows - step if backward else row >= step
        moved_real = jnp.where(kept, pltpu.roll(real, shift, 0), 0.0)
        moved_imag = jnp.where(kept, pltpu.roll(imag, shift, 0), 0.0)
        real, imag = (
            real + mult_real * moved_real - mult_imag * moved_imag,
            imag + mult_imag * moved_real + mult_real * moved_imag,
        )
        mult_real, mult_imag = (
            mult_real * mult_real - mult_imag * mult_imag,
            2.0 * mult_real * mult_imag,
        )
        step *= 2
    return real, imag


def filter_kernel(seen_ref, input_ref, decay_ref, angle_ref, back_decay_ref, back_angle_ref, readout_ref, out_ref):
    modes = decay_ref.shape[1]
    parts = input_ref.shape[1] // seen_ref.shape[1]
    frames = seen_ref.shape[0] // parts
    decay, angle = decay_ref[...], angle_ref[...]
    back_decay, back_angle = back_decay_ref[...], back_angle_ref[...]
    gain = jnp.sqrt(1.0 - decay * decay)
    back_gain = jnp.sqrt(1.0 - back_decay * back_decay)
    seen = jnp.concatenate([seen_ref[pl.ds(k, frames, stride=parts), :] for k in range(parts)], axis=1)
    drive = dot_t(seen, input_ref[...])
    lower, upper = drive[:, :modes], drive[:, modes:]
    lane = lax.broadcasted_iota(jnp.int32, (frames, modes), 1)
    even = lax.rem(2 * lane, modes)
    in_lower = lane < modes // 2
    real = jnp.where(in_lower, lanes_at(lower, even), lanes_at(upper, even)) * gain
    imag = jnp.where(in_lower, lanes_at(lower, even + 1), lanes_at(upper, even + 1)) * gain
    arrived = lax.broadcasted_iota(jnp.int32, real.shape, 0)

    def in_order(part):
        others = jnp.where(arrived < frames // 2, pltpu.roll(part, frames - 1, 0), part)
        return jnp.where(arrived == frames // 2, jnp.broadcast_to(part[:1], part.shape), others)

    real, imag = in_order(real), in_order(imag)
    blocks = lax.axis_size("x")
    row = lax.broadcasted_iota(jnp.int32, (blocks * frames, modes), 0)
    placed = row // frames == lax.axis_index("x")
    real = jnp.where(placed, jnp.concatenate([real] * blocks, axis=0), 0.0)
    imag = jnp.where(placed, jnp.concatenate([imag] * blocks, axis=0), 0.0)
    real, imag = scan_rows(real, imag, decay * jnp.cos(angle), decay * jnp.sin(angle), False)
    real, imag = scan_rows(
        real * back_gain,
        imag * back_gain,
        back_decay * jnp.cos(back_angle),
        back_decay * jnp.sin(back_angle),
        True,
    )
    length = lax.axis_size("z")
    mine = lax.rem(row, length) == lax.axis_index("z")
    shares = out_ref.shape[0] // blocks
    width = readout_ref.shape[0] // shares
    real = jnp.sum(jnp.where(mine, real, 0.0).reshape(blocks, length, modes), axis=1)
    imag = jnp.sum(jnp.where(mine, imag, 0.0).reshape(blocks, length, modes), axis=1)
    if blocks < 8:
        real = jnp.concatenate([real] * (8 // blocks), axis=0)
        imag = jnp.concatenate([imag] * (8 // blocks), axis=0)
    lane = lax.broadcasted_iota(jnp.int32, real.shape, 1)
    mode = lane // 2
    is_real = lane == 2 * mode
    laid = [
        jnp.where(is_real, lanes_at(real, mode + at), lanes_at(imag, mode + at)) for at in (0, modes // 2)
    ]
    latent = dot_t(jnp.concatenate(laid, axis=1), readout_ref[...])
    lanes = out_ref.shape[1]
    for k in range(shares):
        at = k * width
        half = latent[:, at // lanes * lanes : (at // lanes + 1) * lanes]
        turn = (-at) % lanes
        out_ref[pl.ds(k, blocks, stride=shares), :] = (pltpu.roll(half, turn, 1) if turn else half)[:blocks]
    out = out_ref[...]
    first = middle_of(blocks, shares)
    place = lax.broadcasted_iota(jnp.int32, out.shape, 0)
    others = jnp.where(place <= first, pltpu.roll(out, 1, 0), out)
    out_ref[...] = jnp.where(place == 0, jnp.broadcast_to(out[first : first + 1], out.shape), others)


def filter_frames(seen, input_map, mode_decay, mode_angle, smooth_decay, smooth_angle, readout, shares):
    return pl.pallas_call(
        filter_kernel,
        out_shape=jax.ShapeDtypeStruct((lax.axis_size("x") * shares, seen.shape[1]), jnp.float32),
        in_specs=[VMEM] * 7,
        out_specs=VMEM,
        compiler_params=pltpu.CompilerParams(vmem_limit_bytes=8 << 20),
        name="filter_frames",
    )(
        seen,
        input_map,
        mode_decay[None],
        mode_angle[None],
        smooth_decay[None],
        smooth_angle[None],
        readout,
    )


def shards(
    movie_frames,
    patch_weight,
    depth_weight,
    point_weight,
    observe_weight,
    input_map,
    mode_decay,
    mode_angle,
    smooth_decay,
    smooth_angle,
    readout,
):
    tile_count = lax.axis_size("tile")
    partial_value = jnp.dot(
        encode(movie_frames, patch_weight, depth_weight, point_weight).reshape(1, -1),
        observe_weight.reshape(-1, observe_weight.shape[-1]),
        preferred_element_type=jnp.float32,
    )
    length = lax.axis_size("z")
    partial_value = lax.optimization_barrier(partial_value)
    seen = lax.all_to_all(
        jnp.broadcast_to(partial_value.reshape(1, -1, 128), (length, partial_value.shape[1] // 128, 128)),
        "z",
        0,
        0,
        axis_index_groups=[led_by(length, length // 2)],
    ).reshape(-1, 128)
    shares = filter_frames(
        seen, input_map, mode_decay, mode_angle, smooth_decay, smooth_angle, readout, tile_count
    )
    blocks = lax.axis_size("x")
    order = led_by(blocks * tile_count, middle_of(blocks, tile_count))
    terms = lax.all_to_all(shares, ("x", "tile"), 0, 0, axis_index_groups=[order])
    return jnp.sum(terms, axis=0, keepdims=True)[:, : readout.shape[0] // tile_count]


def solution(mesh):
    grid = Mesh(mesh.devices.reshape(BLOCKS, -1, mesh.shape["tile"]), ("x", "z", "tile"))
    placed = (
        P(("x", "z"), None, "tile"),
        P(),
        P(),
        P(),
        P("tile", None, None, None),
        P(),
        P(),
        P(),
        P(),
        P(),
        P(),
    )
    return jax.shard_map(
        shards, mesh=grid, in_specs=placed, out_specs=P(("x", "z"), "tile"), check_vma=False
    )
```

```python
import jax
import jax.numpy as jnp
from jax import lax
from jax.experimental import pallas as pl
from jax.experimental.pallas import tpu as pltpu
from jax.sharding import Mesh
from jax.sharding import PartitionSpec as P

PATCH = 8
POOL = 8
LAYERS = 3
BLOCKS = 4


def led_by(size, first):
    return [first] + [i for i in range(size) if i != first]


def middle_of(blocks, shares):
    return blocks // 2 * shares + shares // 2 + 1


PAD = 8
EDGE = LAYERS
VMEM = pl.BlockSpec(memory_space=pltpu.VMEM)
HBM = pl.BlockSpec(memory_space=pltpu.HBM)
PARTS = 4
CUBIC = 0.044715
ROOT = 0.7978845608028654


def gelu_of_half(y):
    return y + y * jnp.tanh(y * (2.0 * ROOT + (8.0 * ROOT * CUBIC) * (y * y)))


def put_column(ref, at, value):
    rows, lanes = value.shape
    zeros = jnp.zeros((PAD, lanes), ref.dtype)
    ref[at, :PAD, :] = zeros
    ref[at, PAD : PAD + rows, :] = value.astype(ref.dtype)
    ref[at, PAD + rows :, :] = zeros


def put_shifted(column, target):
    half = target.shape[1]
    for dr in range(3):
        at = PAD - 1 + dr
        target[dr] = jnp.concatenate(
            [column[at : at + half, :], column[at + half : at + 2 * half, :]], axis=1
        ).astype(target.dtype)


def embed_kernel(frame_hbm, patch_hbm, depth_hbm, point_hbm, hidden_ref, partner_ref, other_ref, depth_ref,
                 point_ref, frame_ref, weight_ref, first_ref, last_ref, wide_ref, spread_ref, sems):
    height, lanes = frame_ref.shape
    rows = height // PATCH
    channels = weight_ref.shape[1]
    group = 32
    cells = group // PATCH
    columns = lanes // PATCH
    part = height // PARTS
    pieces = [
        pltpu.make_async_copy(
            frame_hbm.at[0, pl.ds(k * part, part), :], frame_ref.at[pl.ds(k * part, part), :], sems.at[k]
        )
        for k in range(PARTS)
    ]
    patch = pltpu.make_async_copy(patch_hbm, weight_ref, sems.at[PARTS])
    depth = pltpu.make_async_copy(depth_hbm, depth_ref, sems.at[PARTS + 1])
    point = pltpu.make_async_copy(point_hbm, point_ref, sems.at[PARTS + 2])
    patch.start()
    for piece in pieces:
        piece.start()
    depth.start()
    point.start()
    spread_ref[...] = jnp.zeros(spread_ref.shape, spread_ref.dtype)
    patch.wait()
    weight = weight_ref[...].astype(jnp.float32) * 0.5
    for i in range(PATCH):
        for c in range(cells):
            at = (i * cells + c) * PATCH
            spread_ref[at : at + PATCH, c * channels : (c + 1) * channels] = weight[i * PATCH : (i + 1) * PATCH]
    spread = spread_ref[...].astype(jnp.bfloat16)
    for k, piece in enumerate(pieces):
        piece.wait()
        wide_ref[pl.ds(k * part, part), :] = frame_ref[pl.ds(k * part, part), :].astype(jnp.float32)
    lines = [wide_ref[pl.ds(i, rows, stride=PATCH), :] for i in range(PATCH)]
    lane_group = lax.broadcasted_iota(jnp.int32, (rows, lanes), 1) // group
    per = lanes // group
    for q in range(per):
        halves = []
        for h in range(PATCH // per):
            half = None
            for s in range(per):
                line = lines[h * per + s]
                shift = ((s - q) * group) % lanes
                line = pltpu.roll(line, shift, 1) if shift else line
                half = line if half is None else jnp.where(lane_group == s, line, half)
            halves.append(half.astype(jnp.bfloat16))
        y = jnp.dot(jnp.concatenate(halves, axis=1), spread, preferred_element_type=jnp.float32)
        for c in range(cells):
            value = gelu_of_half(y[:, c * channels : (c + 1) * channels]).astype(jnp.bfloat16)
            at = q * cells + c
            put_column(hidden_ref, at, value)
            if at < EDGE:
                first_ref[at] = value
            if at >= columns - EDGE:
                last_ref[at - (columns - EDGE)] = value
    odd = lax.rem(lax.axis_index("tile"), 2) == 1
    partner_ref[...] = jnp.where(odd, first_ref[...], last_ref[...])
    other_ref[...] = jnp.where(odd, last_ref[...], first_ref[...])
    depth.wait()
    point.wait()


def embed(frames, patch_weight, depth_weight, point_weight):
    _, height, lanes = frames.shape
    rows, columns, channels = height // PATCH, lanes // PATCH, patch_weight.shape[1]
    edge = jax.ShapeDtypeStruct((EDGE, rows, channels), jnp.bfloat16)
    return pl.pallas_call(
        embed_kernel,
        out_shape=(
            jax.ShapeDtypeStruct((columns, rows + 2 * PAD, channels), jnp.float32),
            edge,
            edge,
            jax.ShapeDtypeStruct(depth_weight.shape, depth_weight.dtype),
            jax.ShapeDtypeStruct(point_weight.shape, point_weight.dtype),
        ),
        in_specs=[HBM] * 4,
        out_specs=(VMEM,) * 5,
        scratch_shapes=[
            pltpu.VMEM((height, lanes), frames.dtype),
            pltpu.VMEM(patch_weight.shape, patch_weight.dtype),
            pltpu.VMEM(edge.shape, edge.dtype),
            pltpu.VMEM(edge.shape, edge.dtype),
            pltpu.VMEM((height, lanes), jnp.float32),
            pltpu.VMEM((256, 4 * channels), jnp.float32),
            pltpu.SemaphoreType.DMA((PARTS + 3,)),
        ],
        compiler_params=pltpu.CompilerParams(vmem_limit_bytes=16 << 20),
        name="embed",
    )(*(pltpu.with_memory_space_constraint(x, pltpu.HBM) for x in (frames, patch_weight, depth_weight, point_weight)))


def taps_of(depth_ref, layer, half):
    channels = depth_ref.shape[3]
    taps = []
    for k in range(9):
        tap = depth_ref[layer, k // 3, k % 3 : k % 3 + 1, :].astype(jnp.float32)
        taps.append(jnp.broadcast_to(jnp.concatenate([tap, tap], axis=1), (half, 2 * channels)).astype(jnp.bfloat16))
    return taps


def weights_of(point_ref, layer):
    weight = point_ref[layer].astype(jnp.float32) * 0.5
    zero = jnp.zeros_like(weight)
    return jnp.concatenate(
        [jnp.concatenate([weight, zero], axis=1), jnp.concatenate([zero, weight], axis=1)], axis=0
    ).astype(jnp.bfloat16)


def new_column(left, middle, right, here, taps, weight):
    half, channels = middle.shape[1], here.shape[1]
    terms = [ref[dr] * taps[3 * dr + dc] for dc, ref in enumerate((left, middle, right)) for dr in range(3)]
    while len(terms) > 1:
        terms = [sum(terms[k : k + 2][1:], terms[k]) for k in range(0, len(terms), 2)]
    y = gelu_of_half(jnp.dot(terms[0], weight, preferred_element_type=jnp.float32))
    y = jnp.concatenate([y[:, :channels], y[:, channels:]], axis=0)
    return here[PAD : PAD + 2 * half, :] + y


def inner_kernel(hidden_ref, depth_ref, point_ref, one_ref, two_ref, sum_ref, shifted_ref):
    columns = hidden_ref.shape[0]
    rows = 2 * shifted_ref.shape[3]
    taps = [taps_of(depth_ref, layer, rows // 2) for layer in range(LAYERS)]
    weights = [weights_of(point_ref, layer) for layer in range(LAYERS)]
    for at in range(columns):
        put_shifted(hidden_ref.at[at], shifted_ref.at[0, at])
    levels = (hidden_ref, one_ref, two_ref, None)
    for layer in range(LAYERS):
        source, target = levels[layer : layer + 2]
        for at in range(layer + 1, columns - layer - 1):
            value = new_column(
                *(shifted_ref.at[layer, at + dc] for dc in (-1, 0, 1)), source.at[at], taps[layer], weights[layer]
            )
            if target is not None:
                put_column(target, at, value)
                put_shifted(target.at[at], shifted_ref.at[layer + 1, at])
            elif at in (EDGE, columns // 2):
                sum_ref[at // POOL] = value
            else:
                sum_ref[at // POOL] += value


def outer_kernel(hidden_ref, one_ref, two_ref, sum_ref, partner_ref, other_ref, depth_ref, point_ref,
                 pooled_ref, border_ref, shifted_ref):
    columns = hidden_ref.shape[0]
    rows = 2 * shifted_ref.shape[4]
    taps = [taps_of(depth_ref, layer, rows // 2) for layer in range(LAYERS)]
    weights = [weights_of(point_ref, layer) for layer in range(LAYERS)]
    here, size = lax.axis_index("tile"), lax.axis_size("tile")
    odd = lax.rem(here, 2)
    inside = ((here > 0).astype(jnp.float32), (here < size - 1).astype(jnp.float32))
    known = (hidden_ref, one_ref, two_ref)

    def border(side, level, at):
        return at + EDGE - level if side == 0 else at - columns + level

    def shifted(side, level, at):
        return shifted_ref.at[side, level, border(side, level, at) + (0 if side == 0 else 2)]

    for level in range(LAYERS):
        for at in (level, level + 1):
            put_shifted(known[level].at[at], shifted(0, level, at))
            mirror = columns - 1 - at
            put_shifted(known[level].at[mirror], shifted(1, level, mirror))
    for halo, side in ((partner_ref, 1 - odd), (other_ref, odd)):
        for k in range(EDGE):
            put_column(border_ref.at[side, 0], k, halo[k].astype(jnp.float32))
    for side in range(2):
        for k in range(EDGE):
            put_shifted(border_ref.at[side, 0, k], shifted_ref.at[side, 0, k + 2 * side])

    sums = [sum_ref[0], sum_ref[1]]
    for layer in range(LAYERS):
        for side in range(2):
            for k in range(EDGE):
                at = k - 2 + layer if side == 0 else columns - 1 - layer + k
                if layer <= at < columns - layer:
                    source = known[layer].at[at]
                else:
                    source = border_ref.at[side, layer, border(side, layer, at)]
                value = new_column(
                    *(shifted(side, layer, at + dc) for dc in (-1, 0, 1)), source, taps[layer], weights[layer]
                )
                if layer == LAYERS - 1:
                    sums[side] = sums[side] + value
                else:
                    if at < 0 or at >= columns:
                        value = value * inside[side]
                    put_column(border_ref.at[side, layer + 1], k, value)
                    put_shifted(border_ref.at[side, layer + 1, k], shifted(side, layer + 1, at))
    for g in range(2):
        pooled_ref[g] = (
            jnp.sum(sums[g].reshape(rows // POOL, POOL, sums[g].shape[1]), axis=1) * (1.0 / (POOL * POOL))
        ).astype(jnp.bfloat16)


def encode(frames, patch_weight, depth_weight, point_weight):
    size = lax.axis_size("tile")
    hidden, partner, other, depth_weight, point_weight = embed(
        frames, patch_weight, depth_weight, point_weight
    )
    pairs = [(i, i + 1) for i in range(1, size - 1, 2)]
    other = lax.ppermute(other, "tile", pairs + [(j, i) for i, j in pairs])
    partner = lax.ppermute(partner, "tile", [(i, i ^ 1) for i in range(size)])
    columns, padded, channels = hidden.shape
    rows = padded - 2 * PAD
    level = jax.ShapeDtypeStruct(hidden.shape, jnp.float32)
    one, two, total = pl.pallas_call(
        inner_kernel,
        out_shape=(level, level, jax.ShapeDtypeStruct((2, rows, channels), jnp.float32)),
        in_specs=[VMEM] * 3,
        out_specs=(VMEM,) * 3,
        scratch_shapes=[pltpu.VMEM((LAYERS, columns, 3, rows // 2, 2 * channels), jnp.bfloat16)],
        compiler_params=pltpu.CompilerParams(vmem_limit_bytes=16 << 20),
        cost_estimate=pl.CostEstimate(flops=400_000_000, bytes_accessed=4_000_000, transcendentals=0),
        name="inner",
    )(hidden, depth_weight, point_weight)
    return pl.pallas_call(
        outer_kernel,
        out_shape=jax.ShapeDtypeStruct((2, rows // POOL, channels), jnp.bfloat16),
        in_specs=[VMEM] * 8,
        out_specs=VMEM,
        scratch_shapes=[
            pltpu.VMEM((2, LAYERS, EDGE, padded, channels), jnp.float32),
            pltpu.VMEM((2, LAYERS, EDGE + 2, 3, rows // 2, 2 * channels), jnp.bfloat16),
        ],
        compiler_params=pltpu.CompilerParams(vmem_limit_bytes=20 << 20),
        name="outer",
    )(hidden, one, two, total, partner, other, depth_weight, point_weight)


def in_two(x):
    high = x.astype(jnp.bfloat16)
    return high, (x - high.astype(jnp.float32)).astype(jnp.bfloat16)


def dot_t(a, b):
    def dot(u, v):
        return lax.dot_general(u, v, (((1,), (1,)), ((), ())), preferred_element_type=jnp.float32)

    a_high, a_low = in_two(a)
    b_high, b_low = in_two(b)
    rows = a.shape[0]
    both = jnp.concatenate([a_high.astype(jnp.float32), a_low.astype(jnp.float32)], axis=0).astype(jnp.bfloat16)
    product = dot(both, b_high)
    return product[rows:] + dot(a_high, b_low) + product[:rows]


def lanes_at(x, index):
    return jnp.take_along_axis(x, index, axis=1, mode="promise_in_bounds")


def scan_rows(real, imag, mult_real, mult_imag, backward):
    rows = real.shape[0]
    row = lax.broadcasted_iota(jnp.int32, real.shape, 0)
    step = 1
    while step < rows:
        shift = rows - step if backward else step
        kept = row < rows - step if backward else row >= step
        moved_real = jnp.where(kept, pltpu.roll(real, shift, 0), 0.0)
        moved_imag = jnp.where(kept, pltpu.roll(imag, shift, 0), 0.0)
        real, imag = (
            real + mult_real * moved_real - mult_imag * moved_imag,
            imag + mult_imag * moved_real + mult_real * moved_imag,
        )
        mult_real, mult_imag = (
            mult_real * mult_real - mult_imag * mult_imag,
            2.0 * mult_real * mult_imag,
        )
        step *= 2
    return real, imag


def filter_kernel(seen_ref, input_ref, decay_ref, angle_ref, back_decay_ref, back_angle_ref, readout_ref, out_ref):
    modes = decay_ref.shape[1]
    parts = input_ref.shape[1] // seen_ref.shape[1]
    frames = seen_ref.shape[0] // parts
    decay, angle = decay_ref[...], angle_ref[...]
    back_decay, back_angle = back_decay_ref[...], back_angle_ref[...]
    gain = jnp.sqrt(1.0 - decay * decay)
    back_gain = jnp.sqrt(1.0 - back_decay * back_decay)
    seen = jnp.concatenate([seen_ref[pl.ds(k, frames, stride=parts), :] for k in range(parts)], axis=1)
    drive = dot_t(seen, input_ref[...])
    lower, upper = drive[:, :modes], drive[:, modes:]
    lane = lax.broadcasted_iota(jnp.int32, (frames, modes), 1)
    even = lax.rem(2 * lane, modes)
    in_lower = lane < modes // 2
    real = jnp.where(in_lower, lanes_at(lower, even), lanes_at(upper, even)) * gain
    imag = jnp.where(in_lower, lanes_at(lower, even + 1), lanes_at(upper, even + 1)) * gain
    arrived = lax.broadcasted_iota(jnp.int32, real.shape, 0)

    def in_order(part):
        others = jnp.where(arrived < frames // 2, pltpu.roll(part, frames - 1, 0), part)
        return jnp.where(arrived == frames // 2, jnp.broadcast_to(part[:1], part.shape), others)

    real, imag = in_order(real), in_order(imag)
    blocks = lax.axis_size("x")
    row = lax.broadcasted_iota(jnp.int32, (blocks * frames, modes), 0)
    placed = row // frames == lax.axis_index("x")
    real = jnp.where(placed, jnp.concatenate([real] * blocks, axis=0), 0.0)
    imag = jnp.where(placed, jnp.concatenate([imag] * blocks, axis=0), 0.0)
    real, imag = scan_rows(real, imag, decay * jnp.cos(angle), decay * jnp.sin(angle), False)
    real, imag = scan_rows(
        real * back_gain,
        imag * back_gain,
        back_decay * jnp.cos(back_angle),
        back_decay * jnp.sin(back_angle),
        True,
    )
    length = lax.axis_size("z")
    mine = lax.rem(row, length) == lax.axis_index("z")
    shares = out_ref.shape[0] // blocks
    width = readout_ref.shape[0] // shares
    real = jnp.sum(jnp.where(mine, real, 0.0).reshape(blocks, length, modes), axis=1)
    imag = jnp.sum(jnp.where(mine, imag, 0.0).reshape(blocks, length, modes), axis=1)
    if blocks < 8:
        real = jnp.concatenate([real] * (8 // blocks), axis=0)
        imag = jnp.concatenate([imag] * (8 // blocks), axis=0)
    lane = lax.broadcasted_iota(jnp.int32, real.shape, 1)
    mode = lane // 2
    is_real = lane == 2 * mode
    laid = [
        jnp.where(is_real, lanes_at(real, mode + at), lanes_at(imag, mode + at)) for at in (0, modes // 2)
    ]
    latent = dot_t(jnp.concatenate(laid, axis=1), readout_ref[...])
    lanes = out_ref.shape[1]
    for k in range(shares):
        at = k * width
        half = latent[:, at // lanes * lanes : (at // lanes + 1) * lanes]
        turn = (-at) % lanes
        out_ref[pl.ds(k, blocks, stride=shares), :] = (pltpu.roll(half, turn, 1) if turn else half)[:blocks]
    out = out_ref[...]
    first = middle_of(blocks, shares)
    place = lax.broadcasted_iota(jnp.int32, out.shape, 0)
    others = jnp.where(place <= first, pltpu.roll(out, 1, 0), out)
    out_ref[...] = jnp.where(place == 0, jnp.broadcast_to(out[first : first + 1], out.shape), others)


def filter_frames(seen, input_map, mode_decay, mode_angle, smooth_decay, smooth_angle, readout, shares):
    return pl.pallas_call(
        filter_kernel,
        out_shape=jax.ShapeDtypeStruct((lax.axis_size("x") * shares, seen.shape[1]), jnp.float32),
        in_specs=[VMEM] * 7,
        out_specs=VMEM,
        compiler_params=pltpu.CompilerParams(vmem_limit_bytes=8 << 20),
        name="filter_frames",
    )(
        seen,
        input_map,
        mode_decay[None],
        mode_angle[None],
        smooth_decay[None],
        smooth_angle[None],
        readout,
    )


def shards(
    movie_frames,
    patch_weight,
    depth_weight,
    point_weight,
    observe_weight,
    input_map,
    mode_decay,
    mode_angle,
    smooth_decay,
    smooth_angle,
    readout,
):
    tile_count = lax.axis_size("tile")
    partial_value = jnp.dot(
        encode(movie_frames, patch_weight, depth_weight, point_weight).reshape(1, -1),
        observe_weight.reshape(-1, observe_weight.shape[-1]),
        preferred_element_type=jnp.float32,
    )
    length = lax.axis_size("z")
    partial_value = lax.optimization_barrier(partial_value)
    seen = lax.all_to_all(
        jnp.broadcast_to(partial_value.reshape(1, -1, 128), (length, partial_value.shape[1] // 128, 128)),
        "z",
        0,
        0,
        axis_index_groups=[led_by(length, length // 2)],
    ).reshape(-1, 128)
    shares = filter_frames(
        seen, input_map, mode_decay, mode_angle, smooth_decay, smooth_angle, readout, tile_count
    )
    blocks = lax.axis_size("x")
    order = led_by(blocks * tile_count, middle_of(blocks, tile_count))
    terms = lax.all_to_all(shares, ("x", "tile"), 0, 0, axis_index_groups=[order])
    return jnp.sum(terms, axis=0, keepdims=True)[:, : readout.shape[0] // tile_count]


def solution(mesh):
    grid = Mesh(mesh.devices.reshape(BLOCKS, -1, mesh.shape["tile"]), ("x", "z", "tile"))
    placed = (
        P(("x", "z"), None, "tile"),
        P(),
        P(),
        P(),
        P("tile", None, None, None),
        P(),
        P(),
        P(),
        P(),
        P(),
        P(),
    )
    return jax.shard_map(
        shards, mesh=grid, in_specs=placed, out_specs=P(("x", "z"), "tile"), check_vma=False
    )
```
